32 devices in a mesh: rows: 8 (over z, x), chan: 4 (over y, core).
Axes of the slice: x: 2, y: 2, z: 4, core: 2. Of those that a mesh axis runs over, the one named last changes fastest.
Arguments:
- pair_act: bfloat16 [128, 768, 768], P('chan', 'rows'), may hold values from -16 to 16
- pair_cot: bfloat16 [128, 768, 768], P('chan', 'rows'), may hold values from -1.5 to 1.5
- contact: int32 [6, 6], replicated, may hold values from 0 to 1, as said below
- ln_gain: float32 [128], replicated, may hold values from 0.5 to 2
- ln_bias: float32 [128], replicated, may hold values from -2 to 2
- left_gate: bfloat16 [128, 128], P(None, 'chan'), may hold values from -0.5 to 0.5
- left_value: bfloat16 [128, 128], P(None, 'chan'), may hold values from -0.5 to 0.5
- right_gate: bfloat16 [128, 128], P(None, 'chan'), may hold values from -0.5 to 0.5
- right_value: bfloat16 [128, 128], P(None, 'chan'), may hold values from -0.5 to 0.5
Outputs:
- pair_grad: bfloat16 [128, 768, 768], P('chan', 'rows')
- gain_grad: float32 [128], P('chan')
- bias_grad: float32 [128], P('chan')
- left_gate_grad: float32 [128, 128], P(None, 'chan')
- left_value_grad: float32 [128, 128], P(None, 'chan')
- right_gate_grad: float32 [128, 128], P(None, 'chan')
- right_value_grad: float32 [128, 128], P(None, 'chan')
The draws below stay inside these ranges and needn't reach their ends.
Inputs may be any that keep to these rules, and one draw needn't show every extreme that they name: `contact`: each block row has 1 to 2 active blocks, its diagonal block always among them; block row 0 has exactly 2.
All inputs are finite; a program needn't handle non-finite values.
Results may differ from the reference program's by a relative error of at most 0.0068.
Values may be sent and summed in bfloat16 or wider, within the bound.
A program may use at most 256 MiB of HBM per device.

```python
import math
import jax
import jax.numpy as jnp
from jax import lax

C = 128
HID = 128
BT = 128
CAP = 2
NTOK = 768
NB = 6


def draw_contact(key, part):
    first_key, second_key = jax.random.split(jax.random.fold_in(key, 7))
    positions = jnp.arange(NB, dtype=jnp.int32)
    counts = jax.random.randint(first_key, (NB,), 1, CAP + 1, dtype=jnp.int32)
    counts = jnp.where(positions == 0, CAP, counts)
    scores = jax.random.randint(second_key, (NB, NB), 0, 1 << 20, dtype=jnp.int32) * NB + positions[None, :]
    scores = jnp.where(positions[:, None] == positions[None, :], (1 << 20) * NB + NB, scores)
    order = jnp.argsort(-scores, axis=1)
    ranks = jnp.argsort(order, axis=1)
    return (ranks < counts[:, None]).astype(jnp.int32)


def draw_pair_act(key, part):
    first_key, second_key = jax.random.split(jax.random.fold_in(key, 11), 2)
    chan_scale = jnp.exp(jax.random.uniform(first_key, (C, 1, 1), jnp.float32, math.log(0.3), math.log(3.0)))
    base = jax.random.normal(second_key, (C, NTOK, NTOK), jnp.float32)
    values = base * chan_scale
    return jnp.clip(values, -16.0, 16.0).astype(jnp.bfloat16)


def block_scale(rng, extent, cuts, least, largest):
    level = 1.0
    for dim, shards_of in cuts:
        heights = jax.random.uniform(jax.random.fold_in(jax.random.fold_in(rng, 6), dim), (shards_of,), jnp.float32, least / len(cuts), largest / len(cuts))
        level = level * jnp.repeat(jnp.exp(heights), extent[dim] // shards_of).reshape((-1,) + (1,) * (len(extent) - 1 - dim))
    return level


def gaussian(own_key, shape, scale, limit, shards=(), kind=jnp.bfloat16):
    result = scale * jax.random.normal(own_key, shape, jnp.float32)
    if shards:
        result = result * block_scale(own_key, shape, shards, -0.22, 0.18)
    return jnp.clip(result, -limit, limit).astype(kind)


def setup_inputs(seed: int = 0) -> dict:
    arg_keys = jax.random.split(jax.random.key(seed), 10)
    return {
        "pair_act": draw_pair_act(jax.random.fold_in(arg_keys[9], 71), 0),
        "pair_cot": gaussian(arg_keys[1], (HID, NTOK, NTOK), 0.25, 1.5, ((0, 4), (1, 8))),
        "contact": draw_contact(jax.random.fold_in(arg_keys[9], 71), 0),
        "ln_gain": jnp.clip(jnp.exp(jax.random.uniform(arg_keys[3], (C,), jnp.float32, math.log(0.5), math.log(2.0))), 0.5, 2.0),
        "ln_bias": gaussian(arg_keys[4], (C,), 0.5, 2.0, (), jnp.float32),
        "left_gate": gaussian(arg_keys[5], (C, HID), C ** -0.5, 0.5, ((1, 4),)),
        "left_value": gaussian(arg_keys[6], (C, HID), C ** -0.5, 0.5, ((1, 4),)),
        "right_gate": gaussian(arg_keys[7], (C, HID), C ** -0.5, 0.5, ((1, 4),)),
        "right_value": gaussian(arg_keys[8], (C, HID), C ** -0.5, 0.5, ((1, 4),)),
    }


EPS = 1e-05

def reference(pair_act, pair_cot, contact, ln_gain, ln_bias, left_gate, left_value, right_gate, right_value):
    block_mask = contact.astype(jnp.float32)
    pair_mask = jnp.repeat(jnp.repeat(block_mask, BT, axis=0), BT, axis=1)
    values = pair_act.astype(jnp.float32)
    mean = lax.optimization_barrier(jnp.mean(values, axis=0))
    inv_std = lax.rsqrt(lax.optimization_barrier(jnp.mean(values * values, axis=0)) - mean * mean + EPS)
    standard = (values - mean) * inv_std
    normed = (standard * ln_gain[:, None, None] + ln_bias[:, None, None]).astype(jnp.bfloat16)
    normed_wide = normed.astype(jnp.float32)

    def project(weight):
        return jnp.einsum('ch,ckn->hkn', weight.astype(jnp.float32), normed_wide)
    left_logit = project(left_gate)
    left_linear = project(left_value)
    right_logit = project(right_gate)
    right_linear = project(right_value)
    left_sigmoid = jax.nn.sigmoid(left_logit)
    right_sigmoid = jax.nn.sigmoid(right_logit)
    left = (pair_mask * left_sigmoid * left_linear).astype(jnp.bfloat16)
    right = (pair_mask * right_sigmoid * right_linear).astype(jnp.bfloat16)
    masked_cot = pair_cot.astype(jnp.float32) * pair_mask
    grad_left = jnp.einsum('hkj,hij->hki', right.astype(jnp.float32), masked_cot)
    grad_right = jnp.einsum('hki,hij->hkj', left.astype(jnp.float32), masked_cot)
    keep_left = grad_left * pair_mask
    keep_right = grad_right * pair_mask
    left_logit_grad = (keep_left * left_linear * left_sigmoid * (1.0 - left_sigmoid)).astype(jnp.bfloat16)
    left_linear_grad = (keep_left * left_sigmoid).astype(jnp.bfloat16)
    right_logit_grad = (keep_right * right_linear * right_sigmoid * (1.0 - right_sigmoid)).astype(jnp.bfloat16)
    right_linear_grad = (keep_right * right_sigmoid).astype(jnp.bfloat16)

    def back(weight, grad):
        return jnp.einsum('ch,hkn->ckn', weight.astype(jnp.float32), grad.astype(jnp.float32))
    normed_grad = back(left_gate, left_logit_grad) + back(left_value, left_linear_grad)
    normed_grad = normed_grad + back(right_gate, right_logit_grad) + back(right_value, right_linear_grad)
    scaled = normed_grad * ln_gain[:, None, None]
    first_mean = lax.optimization_barrier(jnp.mean(scaled, axis=0))
    second_mean = lax.optimization_barrier(jnp.mean(scaled * standard, axis=0))
    pair_grad = ((scaled - first_mean - standard * second_mean) * inv_std).astype(jnp.bfloat16)
    factor = 1.0 / NTOK
    gain_grad = lax.optimization_barrier(jnp.sum(normed_grad * standard, axis=(1, 2))) * factor
    bias_grad = lax.optimization_barrier(jnp.sum(normed_grad, axis=(1, 2))) * factor

    def weight_grad(grad):
        return jnp.einsum('ckn,hkn->ch', normed_wide, grad.astype(jnp.float32)) * factor
    return (pair_grad, gain_grad, bias_grad, weight_grad(left_logit_grad), weight_grad(left_linear_grad), weight_grad(right_logit_grad), weight_grad(right_linear_grad))
```

```python
import functools
import math

import jax
import jax.numpy as jnp
from jax import lax
from jax.experimental import pallas as pl
from jax.experimental.pallas import tpu as pltpu
from jax.sharding import PartitionSpec as P

EPS = 1e-05


def ring_order(count):
    return list(range(0, count, 2)) + list(range(1, count, 2))[::-1]


def flip(x, axis, bit):
    count = lax.axis_size(axis)
    return lax.ppermute(x, axis, [(d, d ^ bit) for d in range(count)])


def bits_down(count):
    bits = [1 << b for b in range(count.bit_length() - 1)]
    return bits[::-1]


def plain(
    pair_act, pair_cot, contact, ln_gain, ln_bias, left_gate, left_value, right_gate, right_value
):
    part_chan, rows_here, width = pair_act.shape
    part_hid = pair_cot.shape[0]
    blocks = contact.shape[0]
    block_len = width // blocks
    chans = lax.axis_size("chan")
    ring = lax.axis_size("rows")
    all_chan = part_chan * chans
    mine = lax.axis_index("chan")
    row_first = lax.axis_index("rows") * rows_here
    piece = math.gcd(rows_here, block_len)
    pieces = rows_here // piece

    numbers = jnp.arange(blocks, dtype=jnp.int32)
    other = jnp.sum(contact * numbers[None, :], axis=1) - numbers
    paired = jnp.sum(contact, axis=1) > 1
    row_block = (row_first + jnp.arange(rows_here, dtype=jnp.int32)) // block_len
    at_own = row_block[:, None] == numbers[None, :]
    row_other = jnp.sum(jnp.where(at_own, other[None, :], 0), axis=1)
    row_paired = jnp.sum(jnp.where(at_own, paired[None, :].astype(jnp.int32), 0), axis=1) > 0
    at_other = (row_other[:, None] == numbers[None, :]) & row_paired[:, None]
    weight = jnp.concatenate(
        [
            jnp.ones((rows_here, block_len), jnp.float32),
            jnp.broadcast_to(
                row_paired.astype(jnp.float32)[:, None], (rows_here, block_len)
            ),
        ],
        axis=1,
    )

    def compact(x):
        def pick(at):
            out = jnp.zeros((x.shape[0], rows_here, block_len), x.dtype)
            for b in range(blocks):
                here = x[:, :, b * block_len : (b + 1) * block_len]
                out = jnp.where(at[:, b][None, :, None], here, out)
            return out

        return jnp.concatenate([pick(at_own), pick(at_other)], axis=2)

    cot = compact(pair_cot)
    own_cot, other_cot = cot[:, :, :block_len], cot[:, :, block_len:]
    order = ring_order(ring)
    place = [order.index(d) for d in range(ring)]
    order_table = jnp.array(order, jnp.int32)
    my_place = jnp.array(place, jnp.int32)[lax.axis_index("rows")]
    right_perm = [(order[i], order[(i + 1) % ring]) for i in range(ring)]
    left_perm = [(order[(i + 1) % ring], order[i]) for i in range(ring)]
    act = compact(pair_act)

    def go_round(x):
        half = x.shape[0] // 2
        top = ring // 2
        arrived = []
        going_right, going_left = x, x
        for step in range(1, top + 1):
            last = step == top and ring % 2 == 0
            if last:
                going_right, going_left = going_right[:half], going_left[half:]
            going_right = lax.ppermute(going_right, "rows", right_perm)
            going_left = lax.ppermute(going_left, "rows", left_perm)
            from_left = order_table[(my_place - step + ring) % ring] * rows_here
            from_right = order_table[(my_place + step) % ring] * rows_here
            arrived.append((going_right, 0, from_left))
            arrived.append((going_left, half if last else 0, from_right))
        here, _ = lax.optimization_barrier((x, arrived[0][0]))
        out = jnp.zeros((x.shape[0], width, x.shape[2]), x.dtype)
        out = lax.dynamic_update_slice(out, here, (0, row_first, 0))
        for block, first, at in arrived:
            out = lax.dynamic_update_slice(out, block, (first, at, 0))
        return out

    gathered = go_round(own_cot)
    reach = -(-(block_len - piece) // rows_here)
    window = [other_cot]
    for hop in range(1, min(reach, ring - 1) + 1):
        up = [(d, d + hop) for d in range(ring - hop)]
        down = [(d + hop, d) for d in range(ring - hop)]
        window = (
            [lax.ppermute(other_cot, "rows", up)]
            + window
            + [lax.ppermute(other_cot, "rows", down)]
        )
    window_first = row_first - (len(window) // 2) * rows_here
    window = jnp.concatenate(window, axis=1)
    owns = [(row_first + p * piece) // block_len for p in range(pieces)]
    seconds = [other[own] for own in owns]
    mutual_row = paired & paired[other] & (other[other] == numbers)

    def crossed(x):
        everywhere = go_round(x)
        return [
            jnp.where(
                mutual_row[own],
                lax.dynamic_slice(
                    everywhere, (0, second * block_len, 0), (part_hid, block_len, block_len)
                ),
                jnp.zeros((), x.dtype),
            )
            for own, second in zip(owns, seconds)
        ]

    def uncrossed(x):
        return [jnp.zeros((part_hid, block_len, block_len), x.dtype) for _ in owns]

    cross = lax.cond(jnp.any(mutual_row), crossed, uncrossed, other_cot)

    parts, offsets = [act], [0]
    for bit in bits_down(chans):
        parts = parts + [flip(x, "chan", bit) for x in parts]
        offsets = offsets + [o + bit for o in offsets]
    full_act = jnp.concatenate(parts, axis=0).astype(jnp.float32)
    partner = jnp.array(offsets, jnp.int32) ^ mine

    def by_partner(x):
        return x.reshape((chans, part_chan) + x.shape[1:])[partner].reshape(x.shape)

    slot_of = [offsets.index(o) for o in range(chans)]
    back_order = jnp.array(slot_of, jnp.int32)[jnp.arange(chans, dtype=jnp.int32) ^ mine]

    def by_channel(x):
        return x.reshape((chans, part_chan) + x.shape[1:])[back_order].reshape(x.shape)

    gain = by_partner(ln_gain)
    bias = by_partner(ln_bias)
    w_stacked = by_partner(
        jnp.concatenate([left_gate, left_value, right_gate, right_value], axis=1)
    )

    mean = jnp.mean(full_act, axis=0)
    inv_std = lax.rsqrt(jnp.mean(full_act * full_act, axis=0) - mean * mean + EPS)
    standard = (full_act - mean) * inv_std
    normed = (standard * gain[:, None, None] + bias[:, None, None]).astype(jnp.bfloat16)
    standard_near = standard.astype(jnp.bfloat16)
    projected = jnp.einsum("ch,ckn->hkn", w_stacked, normed, preferred_element_type=jnp.float32)
    left_logit, left_linear, right_logit, right_linear = jnp.split(projected, 4, axis=0)
    left_sigmoid = jax.nn.sigmoid(left_logit)
    right_sigmoid = jax.nn.sigmoid(right_logit)
    left = (weight * left_sigmoid * left_linear).astype(jnp.bfloat16)
    right = (weight * right_sigmoid * right_linear).astype(jnp.bfloat16)

    corners = []
    for own, second, back_cross in zip(owns, seconds, cross):
        size = (part_hid, block_len, block_len)
        top = jnp.concatenate(
            [
                lax.dynamic_slice(gathered, (0, own * block_len, 0), size),
                lax.dynamic_slice(window, (0, own * block_len - window_first, 0), size),
            ],
            axis=2,
        )
        low = jnp.concatenate(
            [back_cross, lax.dynamic_slice(gathered, (0, second * block_len, 0), size)], axis=2
        )
        corners.append(jnp.concatenate([top, low], axis=1))
    corner = jnp.stack(corners, axis=1)

    def cut(x):
        return x.reshape(part_hid, pieces, piece, 2 * block_len)

    grad_left = jnp.einsum(
        "hpkj,hpij->hpki", cut(right), corner, preferred_element_type=jnp.float32
    ).reshape(left.shape)
    grad_right = jnp.einsum(
        "hpki,hpij->hpkj", cut(left), corner, preferred_element_type=jnp.float32
    ).reshape(left.shape)
    keep_left = grad_left * weight
    keep_right = grad_right * weight
    grads = jnp.concatenate(
        [
            (keep_left * left_linear * left_sigmoid * (1.0 - left_sigmoid)).astype(jnp.bfloat16),
            (keep_left * left_sigmoid).astype(jnp.bfloat16),
            (keep_right * right_linear * right_sigmoid * (1.0 - right_sigmoid)).astype(
                jnp.bfloat16
            ),
            (keep_right * right_sigmoid).astype(jnp.bfloat16),
        ],
        axis=0,
    )

    def back(rows):
        return jnp.einsum("ch,hkn->ckn", rows, grads, preferred_element_type=jnp.float32)

    w_parts = {o: w_stacked[i * part_chan : (i + 1) * part_chan] for i, o in enumerate(offsets)}
    partial = {o: back(w_parts[o]) for o in offsets}
    first_sum = jnp.zeros(mean.shape, jnp.float32)
    second_sum = jnp.zeros(mean.shape, jnp.float32)
    for i, o in enumerate(offsets):
        span = slice(i * part_chan, (i + 1) * part_chan)
        scaled = partial[o] * gain[span][:, None, None]
        first_sum = first_sum + jnp.sum(scaled, axis=0)
        second_sum = second_sum + jnp.sum(scaled * standard[span], axis=0)
    sums = jnp.stack([first_sum, second_sum])
    late_grads = grads
    for bit in bits_down(chans)[::-1]:
        leaving = {o: partial[o].astype(jnp.bfloat16) for o in partial if o & bit}
        received = {o - bit: flip(x, "chan", bit) for o, x in leaving.items()}
        late_grads, _ = lax.optimization_barrier((late_grads, tuple(leaving.values())))
        partial = {o: partial[o] + x.astype(jnp.float32) for o, x in received.items()}
        sums = sums + flip(sums, "chan", bit)
    normed_grad = partial[0]
    scaled = normed_grad * gain[:part_chan][:, None, None]
    pair_grad = (
        (scaled - sums[0] / all_chan - standard[:part_chan] * (sums[1] / all_chan)) * inv_std
    ).astype(jnp.bfloat16)
    near, far = pair_grad[:, :, :block_len], pair_grad[:, :, block_len:]
    none = jnp.zeros((), pair_grad.dtype)
    pair_grad = jnp.concatenate(
        [
            jnp.where(
                at_own[:, b][None, :, None],
                near,
                jnp.where(at_other[:, b][None, :, None], far, none),
            )
            for b in range(blocks)
        ],
        axis=2,
    )

    weight_total = jnp.einsum("ckn,hkn->ch", normed, late_grads, preferred_element_type=jnp.float32)
    moment = jnp.einsum("ckn,hkn->ch", standard_near, late_grads, preferred_element_type=jnp.float32)
    wide = w_stacked.astype(jnp.float32)
    gain_terms = jnp.sum(wide * moment, axis=1)
    bias_terms = jnp.sum(wide * jnp.sum(late_grads.astype(jnp.float32), axis=(1, 2))[None, :], axis=1)
    vectors = by_channel(jnp.stack([gain_terms, bias_terms], axis=1))
    for bit in bits_down(chans):
        vectors = vectors + flip(vectors, "chan", bit)
    vectors = lax.dynamic_slice_in_dim(vectors, mine * part_chan, part_chan, 0)
    for bit in bits_down(ring):
        vectors = vectors + flip(vectors, "rows", bit)
        weight_total = weight_total + flip(weight_total, "rows", bit)
    factor = 1.0 / width
    weight_total = by_channel(weight_total) * factor
    vectors = vectors * factor
    return (pair_grad, vectors[:, 0], vectors[:, 1]) + tuple(jnp.split(weight_total, 4, axis=1))


MESH = pl.DeviceIdType.MESH
VMEM_BYTES = 66 << 20
CHUNKS = 2


def dot(a, b):
    return lax.dot_general(a, b, (((1,), (0,)), ((), ())), preferred_element_type=jnp.float32)


def dot_t(a, b):
    return lax.dot_general(a, b, (((1,), (1,)), ((), ())), preferred_element_type=jnp.float32)


def ring_at(place, ring):
    late = place // (ring // 2)
    return (1 - late) * 2 * place + late * (2 * (ring - 1 - place) + 1)


def ring_place(d, ring):
    return (1 - d % 2) * (d // 2) + (d % 2) * (ring - 1 - d // 2)


def mega(cross, dims, tab, act_hbm, cot_hbm, wt_ref, wb_ref, gain_ref, bias_ref, *rest):
    chans, ring, pc, rows, piece, pieces, blk, width = dims
    if cross:
        cross_hbm, rest = rest[0], rest[1:]
    (
        pg_ref, wsum_ref, vec_ref,
        act_raw, cot_raw, X, Nn, Pm, LR, GX, Dall, Ow, RC, YS, YR, INV, S, SR, SB, SY,
        WA, GA, WS, VS,
        ld, ys, yr, cs, cr, fs, fr, rs, rr, os_, or_, qs, qr, ts, tr, us, ur, zs, zr, wbs, wbr, vs, vr,
    ) = rest[:47]
    if cross:
        BL, GY = rest[47:]
    me = lax.axis_index("rows")
    mine = lax.axis_index("chan")
    core = mine + 1 - 2 * (mine % 2)
    flipped = (mine + chans // 2) % chans
    far = core + 0
    far = (core + chans // 2) % chans
    row_first = me * rows
    place = ring_place(me, ring)
    right = ring_at((place + 1) % ring, ring)
    left = ring_at((place + ring - 1) % ring, ring)
    halves = 2
    owns = [(row_first + p * piece) // blk for p in range(pieces)]
    paired = [tab[1, p].astype(jnp.float32) for p in range(pieces)]

    blocks = width // blk
    picks = [[tab[0, p] == b for b in range(blocks)] for p in range(pieces)]

    def second_of(p, read):
        out = read(0)
        for b in range(1, blocks):
            out = jnp.where(picks[p][b], read(b), out)
        return out

    loads = []
    cot_load = pltpu.make_async_copy(cot_hbm, cot_raw, ld.at[0])
    cot_load.start()
    act_load = pltpu.make_async_copy(act_hbm, act_raw, ld.at[1])
    act_load.start()
    if cross:
        cross_load = pltpu.make_async_copy(cross_hbm, BL, ld.at[2])
        cross_load.start()

    barrier = pltpu.get_barrier_semaphore()
    for hop in range(1, ring):
        pl.semaphore_signal(barrier, inc=1, device_id=((me + hop) % ring, mine), device_id_type=MESH)
    for hop in range(1, chans):
        pl.semaphore_signal(barrier, inc=1, device_id=(me, (mine + hop) % chans), device_id_type=MESH)
    pl.semaphore_wait(barrier, ring - 1 + chans - 1)

    def remote(src, dst, send, recv, r, c):
        return pltpu.make_async_remote_copy(
            src_ref=src, dst_ref=dst, send_sem=send, recv_sem=recv,
            device_id=(r, c), device_id_type=MESH,
        )

    act_load.wait()

    def turn(p):
        def gather_own(c, carry):
            own_col = pl.multiple_of(owns[p] * blk, blk)
            at = pl.ds(pl.multiple_of(c * rows + p * piece, piece), piece)
            span = pl.ds(p * piece, piece)
            LR[0, at, :] = act_raw[c, span, pl.ds(own_col, blk)].astype(jnp.float32)
            LR[1, at, :] = second_of(
                p, lambda b: act_raw[c, span, b * blk : (b + 1) * blk].astype(jnp.float32)
            )
            return carry

        lax.fori_loop(0, pc, gather_own, 0, unroll=4)

        def spread(k, carry):
            for hf in range(halves):
                X[hf, k, mine] = LR[hf, pl.ds(k, pc, stride=rows), :].astype(jnp.bfloat16)
            return carry

        lax.fori_loop(p * piece, (p + 1) * piece, spread, 0, unroll=4)

    def act_slab(p, c):
        return X.at[:, pl.ds(p * piece, piece), c]

    y_copies, c_copies, f_copies = [], [], []
    for p in range(pieces):
        turn(p)
        slab = act_slab(p, mine)
        y = remote(slab, slab, ys.at[p], yr.at[p], me, flipped)
        y.start()
        c = remote(slab, slab, cs.at[p], cr.at[p], me, core)
        c.start()
        y_copies.append(y)
        c_copies.append(c)

    cot_load.wait()

    def pick_cot(h, carry):
        for p in range(pieces):
            span = pl.ds(p * piece, piece)
            own_col = pl.multiple_of(owns[p] * blk, blk)
            at = pl.ds(pl.multiple_of(row_first + p * piece, piece), piece)
            Dall[h, at, :] = cot_raw[h, span, pl.ds(own_col, blk)]
            other = paired[p] * second_of(
                p, lambda b: cot_raw[h, span, b * blk : (b + 1) * blk].astype(jnp.float32)
            )
            Ow[h, pl.ds(rows + p * piece, piece), :] = other.astype(jnp.bfloat16)
        return carry

    def ring_copy(way, step, ch):
        if way == 0:
            unit, to = ring_at((place - (step - 1) + ring) % ring, ring), right
        else:
            unit, to = ring_at((place + (step - 1)) % ring, ring), left
        size = pc // CHUNKS
        view = Dall.at[pl.ds(ch * size, size), pl.ds(pl.multiple_of(unit * rows, rows), rows)]
        return remote(view, view, rs.at[way, step - 1, ch], rr.at[way, step - 1, ch], to, mine)

    top = ring // 2

    def ways_of(step, ch):
        if step < top:
            return [0, 1]
        return [ch % 2]

    def window_copy(way, p):
        to = (me + 1) % ring if way == 0 else (me + ring - 1) % ring
        src = Ow.at[:, pl.ds(rows + p * piece, piece)]
        dst = Ow.at[:, pl.ds((0 if way == 0 else 2 * rows) + p * piece, piece)]
        return remote(src, dst, os_.at[way, p], or_.at[way, p], to, mine)

    def first_own(d):
        return (d * rows) // blk

    def last_own(d):
        return (d * rows + rows - piece) // blk

    def sends_window(way, p):
        if way == 0:
            return (me < ring - 1) & (owns[p] == first_own(me + 1))
        return (me > 0) & (owns[p] == last_own(me - 1))

    def gets_window(way, p):
        if way == 0:
            return (me > 0) & (((me - 1) * rows + p * piece) // blk == first_own(me))
        return (me < ring - 1) & (((me + 1) * rows + p * piece) // blk == last_own(me))

    lax.fori_loop(0, pc, pick_cot, 0, unroll=2)
    for way in (0, 1):
        for p in range(pieces):
            @pl.when(sends_window(way, p))
            def _(way=way, p=p):
                window_copy(way, p).start()
    for ch in range(CHUNKS):
        for way in (0, 1):
            ring_copy(way, 1, ch).start()

    def forward(step, ch):
        for way in (0, 1):
            if way in ways_of(step - 1, ch):
                ring_copy(way, step - 1, ch).wait_recv()
        if step <= top:
            for way in ways_of(step, ch):
                ring_copy(way, step, ch).start()

    inv_chan = 1.0 / (pc * chans)

    def ahead(p):
        def body(k, carry):
            normed = []
            for hf in range(halves):
                x = X[hf, k].reshape(pc * chans, blk).astype(jnp.float32)
                mean = jnp.sum(x, axis=0, keepdims=True) * inv_chan
                square = jnp.sum(x * x, axis=0, keepdims=True) * inv_chan
                inv = lax.rsqrt(square - mean * mean + EPS)
                standard = (x - mean) * inv
                INV[hf, pl.ds(k, 1), :] = inv
                n = (standard * gain_ref[...] + bias_ref[...]).astype(jnp.bfloat16)
                X[hf, k] = standard.astype(jnp.bfloat16).reshape(chans, pc, blk)
                Nn[hf, k] = n.reshape(chans, pc, blk)
                normed.append(n)
            projected = dot(wt_ref[...], jnp.concatenate(normed, axis=1))
            for hf in range(halves):
                part = projected[:, hf * blk : (hf + 1) * blk]
                ls = jax.nn.sigmoid(part[:pc])
                ll = part[pc : 2 * pc]
                rsig = jax.nn.sigmoid(part[2 * pc : 3 * pc])
                rl = part[3 * pc :]
                Pm[hf, k, 0:pc] = ls
                Pm[hf, k, pc : 2 * pc] = ll
                Pm[hf, k, 2 * pc : 3 * pc] = rsig
                Pm[hf, k, 3 * pc :] = rl
                lv, rv = ls * ll, rsig * rl
                if hf == 1:
                    lv, rv = lv * paired[p], rv * paired[p]
                LR[hf, pl.ds(k, pc, stride=rows), :] = lv
                LR[hf, pl.ds(pc * rows + k, pc, stride=rows), :] = rv
            return carry

        lax.fori_loop(p * piece, (p + 1) * piece, body, 0, unroll=2)

    def arrive(p):
        y_copies[p].wait_recv()
        slab = act_slab(p, flipped)
        f = remote(slab, slab, fs.at[p], fr.at[p], me, core)
        f.start()
        f_copies.append(f)
        c_copies[p].wait_recv()
        f.wait_recv()
        y_copies[p].wait_send()
        c_copies[p].wait_send()
        f.wait_send()

    arrive(0)
    ahead(0)
    forward(2, 0)
    forward(2, 1)
    if pieces > 1:
        arrive(1)
        ahead(1)
    forward(3, 0)
    for p in range(2, pieces):
        arrive(p)
        ahead(p)
    forward(3, 1)

    for way in (0, 1):
        for p in range(pieces):
            @pl.when(gets_window(way, p))
            def _(way=way, p=p):
                window_copy(way, p).wait_recv()
    for step in range(4, top + 1):
        forward(step, 0)
        forward(step, 1)
    if cross:
        cross_load.wait()

    def lr_rows(which, h, p):
        return pl.ds(pl.multiple_of((which * pc + h) * rows + p * piece, piece), piece)

    def near(h, carry):
        for p in range(pieces):
            own_at = pl.ds(pl.multiple_of(owns[p] * blk, blk), blk)
            win_at = pl.ds(pl.multiple_of(owns[p] * blk - row_first + rows, piece), blk)
            tl, tri = Dall[h, own_at, :], Ow[h, win_at, :]
            l0 = LR[0, lr_rows(0, h, p), :].astype(jnp.bfloat16)
            r0 = LR[0, lr_rows(1, h, p), :].astype(jnp.bfloat16)
            r1 = LR[1, lr_rows(1, h, p), :].astype(jnp.bfloat16)
            gl = dot_t(r0, tl) + dot_t(r1, tri)
            gr = dot(l0, jnp.concatenate([tl, tri], axis=1))
            at = pl.ds(pl.multiple_of(h * rows + p * piece, piece), piece)
            gr0 = gr[:, :blk]
            if cross:
                l1 = LR[1, lr_rows(0, h, p), :].astype(jnp.bfloat16)
                gr0 = gr0 + dot(l1, BL[h, p])
                GY[at, :] = dot_t(r0, BL[h, p])
            LR[0, lr_rows(0, h, p), :] = gl
            LR[0, lr_rows(1, h, p), :] = gr0
            GX[at, :] = gr[:, blk:]
        return carry

    lax.fori_loop(0, pc, near, 0)

    def distant(h, carry):
        for p in range(pieces):
            br = second_of(p, lambda b: Dall[h, b * blk : (b + 1) * blk, :])
            l1 = LR[1, lr_rows(0, h, p), :].astype(jnp.bfloat16)
            r1 = LR[1, lr_rows(1, h, p), :].astype(jnp.bfloat16)
            at = pl.ds(pl.multiple_of(h * rows + p * piece, piece), piece)
            gl = dot_t(r1, br)
            if cross:
                gl = gl + GY[at, :]
            LR[1, lr_rows(0, h, p), :] = gl
            LR[1, lr_rows(1, h, p), :] = GX[at, :] + dot(l1, br)
        return carry

    WA[...] = jnp.zeros_like(WA)
    GA[...] = jnp.zeros_like(GA)

    def back(hf, p):
        def body(i, carry):
            grads, total = [], None
            for u in range(2):
                k = p * piece + 2 * i + u
                gl = LR[hf, pl.ds(k, pc, stride=rows), :]
                gr = LR[hf, pl.ds(pc * rows + k, pc, stride=rows), :]
                if hf == 1:
                    gl, gr = gl * paired[p], gr * paired[p]
                ls, ll = Pm[hf, k, 0:pc], Pm[hf, k, pc : 2 * pc]
                rsig, rl = Pm[hf, k, 2 * pc : 3 * pc], Pm[hf, k, 3 * pc :]
                a, b = gl * ls, gr * rsig
                g = jnp.concatenate([a * ll * (1.0 - ls), a, b * rl * (1.0 - rsig), b], axis=0)
                total = g if total is None else total + g
                grads.append(g.astype(jnp.bfloat16))
            GA[...] += total
            pair = jnp.concatenate(grads, axis=1)
            partial = dot(wb_ref[...], pair)
            both = []
            for u in range(2):
                k = p * piece + 2 * i + u
                n = partial[:, u * blk : (u + 1) * blk]
                st = X[hf, k].reshape(pc * chans, blk)
                scaled = n * gain_ref[...]
                S[hf, 0, pl.ds(k, 1), :] = jnp.sum(scaled, axis=0, keepdims=True)
                S[hf, 1, pl.ds(k, 1), :] = jnp.sum(scaled * st.astype(jnp.float32), axis=0, keepdims=True)
                both.append(jnp.concatenate([Nn[hf, k].reshape(pc * chans, blk), st], axis=0))
                Nn[hf, k] = n.astype(jnp.bfloat16).reshape(chans, pc, blk)
            WA[...] += dot_t(jnp.concatenate(both, axis=1), pair)
            return carry

        lax.fori_loop(0, piece // 2, body, 0)

    def span_of(p):
        return pl.ds(p * piece, piece)

    def core_copies(hf, p):
        at = span_of(p)
        return [
            remote(Nn.at[hf, at, core], RC.at[0, hf, at], qs.at[hf, p, 0], qr.at[hf, p, 0], me, core),
            remote(Nn.at[hf, at, far], RC.at[1, hf, at], qs.at[hf, p, 1], qr.at[hf, p, 1], me, core),
            remote(S.at[hf, :, at], SR.at[hf, :, at], ts.at[hf, p], tr.at[hf, p], me, core),
        ]

    def y_back(hf, p):
        at = span_of(p)
        return [
            remote(YS.at[hf, at], YR.at[hf, at], us.at[hf, p], ur.at[hf, p], me, flipped),
            remote(SB.at[hf, :, at], SY.at[hf, :, at], zs.at[hf, p], zr.at[hf, p], me, flipped),
        ]

    def combine(hf, p):
        for c in core_copies(hf, p):
            c.wait_recv()
        at = span_of(p)
        YS[hf, at] = (
            Nn[hf, at, flipped].astype(jnp.float32) + RC[1, hf, at].astype(jnp.float32)
        ).astype(jnp.bfloat16)
        total = S[hf, :, at, :] + SR[hf, :, at, :]
        SR[hf, :, at, :] = total
        SB[hf, :, at, :] = total.astype(jnp.bfloat16)
        for c in y_back(hf, p):
            c.start()

    scale = 1.0 / (pc * chans)

    def finish(hf, p):
        for c in y_back(hf, p):
            c.wait_recv()
        at = span_of(p)
        SR[hf, :, at, :] = (SR[hf, :, at, :] + SY[hf, :, at, :].astype(jnp.float32)) * scale
        gain = gain_ref[pl.ds(pl.multiple_of(mine * pc, pc), pc), :]

        def body(k, carry):
            n = (
                Nn[hf, k, mine].astype(jnp.float32)
                + RC[0, hf, k].astype(jnp.float32)
                + YR[hf, k].astype(jnp.float32)
            )
            st = X[hf, k, mine].astype(jnp.float32)
            s0 = SR[hf, 0, pl.ds(k, 1), :]
            s1 = SR[hf, 1, pl.ds(k, 1), :]
            out = (n * gain - s0 - st * s1) * INV[hf, pl.ds(k, 1), :]
            LR[hf, pl.ds(k, pc, stride=rows), :] = out
            return carry

        lax.fori_loop(p * piece, (p + 1) * piece, body, 0, unroll=4)

        def put(c, carry):
            rows_at = pl.ds(pl.multiple_of(c * rows + p * piece, piece), piece)
            pg_ref[hf, c, at, :] = LR[hf, rows_at, :].astype(jnp.bfloat16)
            return carry

        lax.fori_loop(0, pc, put, 0, unroll=4)

    items = [(hf, p) for hf in range(halves) for p in range(pieces)]
    pending = None
    for hf, p in items:
        if hf == 1 and p == 0:
            forward(top + 1, 0)
            forward(top + 1, 1)
            lax.fori_loop(0, pc, distant, 0)
        back(hf, p)
        for c in core_copies(hf, p):
            c.start()
        if pending is not None:
            combine(*pending)
        pending = (hf, p)
    combine(*pending)

    wide = wb_ref[...].astype(jnp.float32)
    gain_term = jnp.sum(wide * WA[pc * chans :, :], axis=1, keepdims=True)
    bias_term = jnp.sum(
        lax.dot_general(
            wide, GA[...], (((1,), (0,)), ((), ())),
            precision=lax.Precision.HIGHEST, preferred_element_type=jnp.float32,
        ),
        axis=1, keepdims=True,
    )
    lane = lax.broadcasted_iota(jnp.int32, (pc * chans, blk), 1)
    both = jnp.where(lane == 0, gain_term, jnp.where(lane == 1, bias_term, 0.0))
    WS[me, : pc * chans, :] = WA[: pc * chans, :]
    WS[me, pc * chans :, :] = jnp.transpose(both)[:8]

    def wide_copy(hop):
        return remote(
            WS.at[me], WS.at[me], wbs.at[hop - 1], wbr.at[hop - 1], (me + hop) % ring, mine
        )

    for hop in range(1, ring):
        wide_copy(hop).start()

    for p in range(pieces):
        finish(0, p)

    for hop in range(1, ring):
        wide_copy(hop).wait_recv()
    summed = WS[0]
    for d in range(1, ring):
        summed = summed + WS[d]
    summed = summed * (1.0 / width)
    wsum_ref[...] = summed[: pc * chans]
    VS[mine] = summed[pc * chans :]

    def vec_copy(hop):
        return remote(VS.at[mine], VS.at[mine], vs.at[hop - 1], vr.at[hop - 1], me, (mine + hop) % chans)

    for hop in range(1, chans):
        vec_copy(hop).start()
    for p in range(pieces):
        finish(1, p)
    for hop in range(1, chans):
        vec_copy(hop).wait_recv()
    total = VS[0]
    for d in range(1, chans):
        total = total + VS[d]
    vec_ref[...] = total

    for way in (0, 1):
        for p in range(pieces):
            @pl.when(sends_window(way, p))
            def _(way=way, p=p):
                window_copy(way, p).wait_send()
    for step in range(1, top + 1):
        for ch in range(CHUNKS):
            for way in ways_of(step, ch):
                ring_copy(way, step, ch).wait_send()
    for hf, p in items:
        for c in core_copies(hf, p) + y_back(hf, p):
            c.wait_send()
    for hop in range(1, ring):
        wide_copy(hop).wait_send()
    for hop in range(1, chans):
        vec_copy(hop).wait_send()


def call_mega(cross, dims, tab, act, cot, wt, wb, gain, bias, *extra):
    chans, ring, pc, rows, piece, pieces, blk, width = dims
    allc = pc * chans
    bf, f32 = jnp.bfloat16, jnp.float32
    V, D = pltpu.VMEM, pltpu.SemaphoreType.DMA
    top = ring // 2
    scratch = [
        V((pc, rows, width), bf), V((pc, rows, width), bf),
        V((2, rows, chans, pc, blk), bf), V((2, rows, chans, pc, blk), bf),
        V((2, rows, 4 * pc, blk), f32), V((2, 2 * pc * rows, blk), f32), V((pc * rows, blk), f32),
        V((pc, ring * rows, blk), bf), V((pc, 3 * rows, blk), bf),
        V((2, 2, rows, pc, blk), bf), V((2, rows, pc, blk), bf), V((2, rows, pc, blk), bf),
        V((2, rows, blk), f32), V((2, 2, rows, blk), f32), V((2, 2, rows, blk), f32),
        V((2, 2, rows, blk), bf), V((2, 2, rows, blk), bf),
        V((2 * allc, 4 * pc), f32), V((4 * pc, blk), f32),
        V((ring, allc + 8, 4 * pc), f32), V((chans, 8, 4 * pc), f32),
        D((3,)), D((pieces,)), D((pieces,)), D((pieces,)), D((pieces,)), D((pieces,)), D((pieces,)),
        D((2, top, CHUNKS)), D((2, top, CHUNKS)), D((2, pieces)), D((2, pieces)),
        D((2, pieces, 2)), D((2, pieces, 2)), D((2, pieces)), D((2, pieces)),
        D((2, pieces)), D((2, pieces)), D((2, pieces)), D((2, pieces)),
        D((ring - 1,)), D((ring - 1,)), D((chans - 1,)), D((chans - 1,)),
    ]
    if cross:
        scratch += [V((pc, pieces, blk, blk), bf), V((pc * rows, blk), f32)]
    vmem = pl.BlockSpec(memory_space=pltpu.VMEM)
    hbm = pl.BlockSpec(memory_space=pl.ANY)
    return pl.pallas_call(
        functools.partial(mega, cross, dims),
        out_shape=(
            jax.ShapeDtypeStruct((2, pc, rows, blk), bf),
            jax.ShapeDtypeStruct((allc, 4 * pc), f32),
            jax.ShapeDtypeStruct((8, 4 * pc), f32),
        ),
        in_specs=[pl.BlockSpec(memory_space=pltpu.SMEM), hbm, hbm, vmem, vmem, vmem, vmem]
        + [hbm] * len(extra),
        out_specs=(vmem, vmem, vmem),
        scratch_shapes=scratch,
        compiler_params=pltpu.CompilerParams(
            collective_id=2 if cross else 1, has_side_effects=True, vmem_limit_bytes=VMEM_BYTES
        ),
        name="triangle_cross" if cross else "triangle",
    )(tab, act, cot, wt, wb, gain, bias, *extra)


def fused(
    pair_act, pair_cot, contact, ln_gain, ln_bias, left_gate, left_value, right_gate, right_value
):
    pc, rows, width = pair_act.shape
    blocks = contact.shape[0]
    blk = width // blocks
    chans, ring = lax.axis_size("chan"), lax.axis_size("rows")
    piece = math.gcd(rows, blk)
    pieces = rows // piece
    dims = (chans, ring, pc, rows, piece, pieces, blk, width)
    row_first = lax.axis_index("rows") * rows

    numbers = jnp.arange(blocks, dtype=jnp.int32)
    paired = jnp.sum(contact, axis=1) > 1
    other = jnp.where(paired, jnp.sum(contact * numbers[None, :], axis=1) - numbers, numbers)
    owns = (row_first + jnp.arange(pieces, dtype=jnp.int32) * piece) // blk
    at_piece = owns[:, None] == numbers[None, :]

    def of_piece(x):
        return jnp.sum(jnp.where(at_piece, x[None, :].astype(jnp.int32), 0), axis=1)

    tab = jnp.stack([of_piece(other), of_piece(paired)])
    mutual = jnp.sum(contact * contact.T * (numbers[:, None] != numbers[None, :])) > 0

    stacked = jnp.concatenate([left_gate, left_value, right_gate, right_value], axis=1)
    wide = (pc * chans, blk)
    args = (
        tab, pair_act, pair_cot, stacked.T, stacked,
        jnp.broadcast_to(ln_gain[:, None], wide), jnp.broadcast_to(ln_bias[:, None], wide),
    )

    def simple(args):
        return call_mega(False, dims, *args)

    def crossed(args):
        tab, cot = args[0], args[2]
        seconds = [tab[0, p] for p in range(pieces)]
        mine = jnp.concatenate(
            [
                lax.dynamic_slice(
                    cot, (0, p * piece, seconds[p] * blk), (pc, piece, blk)
                )
                for p in range(pieces)
            ],
            axis=1,
        )
        every = lax.all_gather(mine, "rows", axis=1, tiled=True)
        corners = []
        for p in range(pieces):
            own, second = owns[p], seconds[p]
            back = jnp.sum(jnp.where(numbers == second, other, 0))
            good = (tab[1, p] > 0) & (back == own) & (second != own)
            here = lax.dynamic_slice(every, (0, second * blk, 0), (pc, blk, blk))
            corners.append(jnp.where(good, here, jnp.zeros((), here.dtype)))
        return call_mega(True, dims, *args, jnp.stack(corners, axis=1))

    pg, wsum, vec = lax.cond(mutual, crossed, simple, args)

    near, far = pg[0], pg[1]
    none = jnp.zeros((), pg.dtype)
    row_block = (row_first + jnp.arange(rows, dtype=jnp.int32)) // blk
    at_row = row_block[:, None] == numbers[None, :]
    row_other = jnp.sum(jnp.where(at_row, other[None, :], 0), axis=1)
    pair_grad = jnp.concatenate(
        [
            jnp.where(
                at_row[:, b][None, :, None],
                near,
                jnp.where((row_other == b)[None, :, None], far, none),
            )
            for b in range(blocks)
        ],
        axis=2,
    )
    here = lax.axis_index("chan") * pc
    gain_grad = lax.dynamic_slice(vec[0], (here,), (pc,))
    bias_grad = lax.dynamic_slice(vec[1], (here,), (pc,))
    return (pair_grad, gain_grad, bias_grad) + tuple(
        wsum[:, i * pc : (i + 1) * pc] for i in range(4)
    )


def local(*arrays):
    pc, rows, width = arrays[0].shape
    blk = width // arrays[2].shape[0]
    piece = math.gcd(rows, blk)
    chans, ring = lax.axis_size("chan"), lax.axis_size("rows")
    fits = (
        piece % 16 == 0 and rows // piece == 3 and blk == pc * chans == 4 * pc and ring == 8
    )
    return fused(*arrays) if fits else plain(*arrays)


def solution(mesh):
    in_specs = (
        P("chan", "rows", None),
        P("chan", "rows", None),
        P(),
        P(),
        P(),
        P(None, "chan"),
        P(None, "chan"),
        P(None, "chan"),
        P(None, "chan"),
    )
    out_specs = (
        P("chan", "rows", None),
        P("chan"),
        P("chan"),
        P(None, "chan"),
        P(None, "chan"),
        P(None, "chan"),
        P(None, "chan"),
    )
    return jax.shard_map(local, mesh=mesh, in_specs=in_specs, out_specs=out_specs, check_vma=False)
```

```python
import functools
import math

import jax
import jax.numpy as jnp
from jax import lax
from jax.experimental import pallas as pl
from jax.experimental.pallas import tpu as pltpu
from jax.sharding import PartitionSpec as P

EPS = 1e-05


def ring_order(count):
    return list(range(0, count, 2)) + list(range(1, count, 2))[::-1]


def flip(x, axis, bit):
    count = lax.axis_size(axis)
    return lax.ppermute(x, axis, [(d, d ^ bit) for d in range(count)])


def bits_down(count):
    bits = [1 << b for b in range(count.bit_length() - 1)]
    return bits[::-1]


def plain(
    pair_act, pair_cot, contact, ln_gain, ln_bias, left_gate, left_value, right_gate, right_value
):
    part_chan, rows_here, width = pair_act.shape
    part_hid = pair_cot.shape[0]
    blocks = contact.shape[0]
    block_len = width // blocks
    chans = lax.axis_size("chan")
    ring = lax.axis_size("rows")
    all_chan = part_chan * chans
    mine = lax.axis_index("chan")
    row_first = lax.axis_index("rows") * rows_here
    piece = math.gcd(rows_here, block_len)
    pieces = rows_here // piece

    numbers = jnp.arange(blocks, dtype=jnp.int32)
    other = jnp.sum(contact * numbers[None, :], axis=1) - numbers
    paired = jnp.sum(contact, axis=1) > 1
    row_block = (row_first + jnp.arange(rows_here, dtype=jnp.int32)) // block_len
    at_own = row_block[:, None] == numbers[None, :]
    row_other = jnp.sum(jnp.where(at_own, other[None, :], 0), axis=1)
    row_paired = jnp.sum(jnp.where(at_own, paired[None, :].astype(jnp.int32), 0), axis=1) > 0
    at_other = (row_other[:, None] == numbers[None, :]) & row_paired[:, None]
    weight = jnp.concatenate(
        [
            jnp.ones((rows_here, block_len), jnp.float32),
            jnp.broadcast_to(
                row_paired.astype(jnp.float32)[:, None], (rows_here, block_len)
            ),
        ],
        axis=1,
    )

    def compact(x):
        def pick(at):
            out = jnp.zeros((x.shape[0], rows_here, block_len), x.dtype)
            for b in range(blocks):
                here = x[:, :, b * block_len : (b + 1) * block_len]
                out = jnp.where(at[:, b][None, :, None], here, out)
            return out

        return jnp.concatenate([pick(at_own), pick(at_other)], axis=2)

    cot = compact(pair_cot)
    own_cot, other_cot = cot[:, :, :block_len], cot[:, :, block_len:]
    order = ring_order(ring)
    place = [order.index(d) for d in range(ring)]
    order_table = jnp.array(order, jnp.int32)
    my_place = jnp.array(place, jnp.int32)[lax.axis_index("rows")]
    right_perm = [(order[i], order[(i + 1) % ring]) for i in range(ring)]
    left_perm = [(order[(i + 1) % ring], order[i]) for i in range(ring)]
    act = compact(pair_act)

    def go_round(x):
        half = x.shape[0] // 2
        top = ring // 2
        arrived = []
        going_right, going_left = x, x
        for step in range(1, top + 1):
            last = step == top and ring % 2 == 0
            if last:
                going_right, going_left = going_right[:half], going_left[half:]
            going_right = lax.ppermute(going_right, "rows", right_perm)
            going_left = lax.ppermute(going_left, "rows", left_perm)
            from_left = order_table[(my_place - step + ring) % ring] * rows_here
            from_right = order_table[(my_place + step) % ring] * rows_here
            arrived.append((going_right, 0, from_left))
            arrived.append((going_left, half if last else 0, from_right))
        here, _ = lax.optimization_barrier((x, arrived[0][0]))
        out = jnp.zeros((x.shape[0], width, x.shape[2]), x.dtype)
        out = lax.dynamic_update_slice(out, here, (0, row_first, 0))
        for block, first, at in arrived:
            out = lax.dynamic_update_slice(out, block, (first, at, 0))
        return out

    gathered = go_round(own_cot)
    reach = -(-(block_len - piece) // rows_here)
    window = [other_cot]
    for hop in range(1, min(reach, ring - 1) + 1):
        up = [(d, d + hop) for d in range(ring - hop)]
        down = [(d + hop, d) for d in range(ring - hop)]
        window = (
            [lax.ppermute(other_cot, "rows", up)]
            + window
            + [lax.ppermute(other_cot, "rows", down)]
        )
    window_first = row_first - (len(window) // 2) * rows_here
    window = jnp.concatenate(window, axis=1)
    owns = [(row_first + p * piece) // block_len for p in range(pieces)]
    seconds = [other[own] for own in owns]
    mutual_row = paired & paired[other] & (other[other] == numbers)

    def crossed(x):
        everywhere = go_round(x)
        return [
            jnp.where(
                mutual_row[own],
                lax.dynamic_slice(
                    everywhere, (0, second * block_len, 0), (part_hid, block_len, block_len)
                ),
                jnp.zeros((), x.dtype),
            )
            for own, second in zip(owns, seconds)
        ]

    def uncrossed(x):
        return [jnp.zeros((part_hid, block_len, block_len), x.dtype) for _ in owns]

    cross = lax.cond(jnp.any(mutual_row), crossed, uncrossed, other_cot)

    parts, offsets = [act], [0]
    for bit in bits_down(chans):
        parts = parts + [flip(x, "chan", bit) for x in parts]
        offsets = offsets + [o + bit for o in offsets]
    full_act = jnp.concatenate(parts, axis=0).astype(jnp.float32)
    partner = jnp.array(offsets, jnp.int32) ^ mine

    def by_partner(x):
        return x.reshape((chans, part_chan) + x.shape[1:])[partner].reshape(x.shape)

    slot_of = [offsets.index(o) for o in range(chans)]
    back_order = jnp.array(slot_of, jnp.int32)[jnp.arange(chans, dtype=jnp.int32) ^ mine]

    def by_channel(x):
        return x.reshape((chans, part_chan) + x.shape[1:])[back_order].reshape(x.shape)

    gain = by_partner(ln_gain)
    bias = by_partner(ln_bias)
    w_stacked = by_partner(
        jnp.concatenate([left_gate, left_value, right_gate, right_value], axis=1)
    )

    mean = jnp.mean(full_act, axis=0)
    inv_std = lax.rsqrt(jnp.mean(full_act * full_act, axis=0) - mean * mean + EPS)
    standard = (full_act - mean) * inv_std
    normed = (standard * gain[:, None, None] + bias[:, None, None]).astype(jnp.bfloat16)
    standard_near = standard.astype(jnp.bfloat16)
    projected = jnp.einsum("ch,ckn->hkn", w_stacked, normed, preferred_element_type=jnp.float32)
    left_logit, left_linear, right_logit, right_linear = jnp.split(projected, 4, axis=0)
    left_sigmoid = jax.nn.sigmoid(left_logit)
    right_sigmoid = jax.nn.sigmoid(right_logit)
    left = (weight * left_sigmoid * left_linear).astype(jnp.bfloat16)
    right = (weight * right_sigmoid * right_linear).astype(jnp.bfloat16)

    corners = []
    for own, second, back_cross in zip(owns, seconds, cross):
        size = (part_hid, block_len, block_len)
        top = jnp.concatenate(
            [
                lax.dynamic_slice(gathered, (0, own * block_len, 0), size),
                lax.dynamic_slice(window, (0, own * block_len - window_first, 0), size),
            ],
            axis=2,
        )
        low = jnp.concatenate(
            [back_cross, lax.dynamic_slice(gathered, (0, second * block_len, 0), size)], axis=2
        )
        corners.append(jnp.concatenate([top, low], axis=1))
    corner = jnp.stack(corners, axis=1)

    def cut(x):
        return x.reshape(part_hid, pieces, piece, 2 * block_len)

    grad_left = jnp.einsum(
        "hpkj,hpij->hpki", cut(right), corner, preferred_element_type=jnp.float32
    ).reshape(left.shape)
    grad_right = jnp.einsum(
        "hpki,hpij->hpkj", cut(left), corner, preferred_element_type=jnp.float32
    ).reshape(left.shape)
    keep_left = grad_left * weight
    keep_right = grad_right * weight
    grads = jnp.concatenate(
        [
            (keep_left * left_linear * left_sigmoid * (1.0 - left_sigmoid)).astype(jnp.bfloat16),
            (keep_left * left_sigmoid).astype(jnp.bfloat16),
            (keep_right * right_linear * right_sigmoid * (1.0 - right_sigmoid)).astype(
                jnp.bfloat16
            ),
            (keep_right * right_sigmoid).astype(jnp.bfloat16),
        ],
        axis=0,
    )

    def back(rows):
        return jnp.einsum("ch,hkn->ckn", rows, grads, preferred_element_type=jnp.float32)

    w_parts = {o: w_stacked[i * part_chan : (i + 1) * part_chan] for i, o in enumerate(offsets)}
    partial = {o: back(w_parts[o]) for o in offsets}
    first_sum = jnp.zeros(mean.shape, jnp.float32)
    second_sum = jnp.zeros(mean.shape, jnp.float32)
    for i, o in enumerate(offsets):
        span = slice(i * part_chan, (i + 1) * part_chan)
        scaled = partial[o] * gain[span][:, None, None]
        first_sum = first_sum + jnp.sum(scaled, axis=0)
        second_sum = second_sum + jnp.sum(scaled * standard[span], axis=0)
    sums = jnp.stack([first_sum, second_sum])
    late_grads = grads
    for bit in bits_down(chans)[::-1]:
        leaving = {o: partial[o].astype(jnp.bfloat16) for o in partial if o & bit}
        received = {o - bit: flip(x, "chan", bit) for o, x in leaving.items()}
        late_grads, _ = lax.optimization_barrier((late_grads, tuple(leaving.values())))
        partial = {o: partial[o] + x.astype(jnp.float32) for o, x in received.items()}
        sums = sums + flip(sums, "chan", bit)
    normed_grad = partial[0]
    scaled = normed_grad * gain[:part_chan][:, None, None]
    pair_grad = (
        (scaled - sums[0] / all_chan - standard[:part_chan] * (sums[1] / all_chan)) * inv_std
    ).astype(jnp.bfloat16)
    near, far = pair_grad[:, :, :block_len], pair_grad[:, :, block_len:]
    none = jnp.zeros((), pair_grad.dtype)
    pair_grad = jnp.concatenate(
        [
            jnp.where(
                at_own[:, b][None, :, None],
                near,
                jnp.where(at_other[:, b][None, :, None], far, none),
            )
            for b in range(blocks)
        ],
        axis=2,
    )

    weight_total = jnp.einsum("ckn,hkn->ch", normed, late_grads, preferred_element_type=jnp.float32)
    moment = jnp.einsum("ckn,hkn->ch", standard_near, late_grads, preferred_element_type=jnp.float32)
    wide = w_stacked.astype(jnp.float32)
    gain_terms = jnp.sum(wide * moment, axis=1)
    bias_terms = jnp.sum(wide * jnp.sum(late_grads.astype(jnp.float32), axis=(1, 2))[None, :], axis=1)
    vectors = by_channel(jnp.stack([gain_terms, bias_terms], axis=1))
    for bit in bits_down(chans):
        vectors = vectors + flip(vectors, "chan", bit)
    vectors = lax.dynamic_slice_in_dim(vectors, mine * part_chan, part_chan, 0)
    for bit in bits_down(ring):
        vectors = vectors + flip(vectors, "rows", bit)
        weight_total = weight_total + flip(weight_total, "rows", bit)
    factor = 1.0 / width
    weight_total = by_channel(weight_total) * factor
    vectors = vectors * factor
    return (pair_grad, vectors[:, 0], vectors[:, 1]) + tuple(jnp.split(weight_total, 4, axis=1))


MESH = pl.DeviceIdType.MESH
VMEM_BYTES = 66 << 20
CHUNKS = 2


def dot(a, b):
    return lax.dot_general(a, b, (((1,), (0,)), ((), ())), preferred_element_type=jnp.float32)


def dot_t(a, b):
    return lax.dot_general(a, b, (((1,), (1,)), ((), ())), preferred_element_type=jnp.float32)


def ring_at(place, ring):
    late = place // (ring // 2)
    return (1 - late) * 2 * place + late * (2 * (ring - 1 - place) + 1)


def ring_place(d, ring):
    return (1 - d % 2) * (d // 2) + (d % 2) * (ring - 1 - d // 2)


def mega(cross, dims, contact_ref, act_hbm, cot_hbm, lg_ref, lv_ref, rg_ref, rv_ref, g_ref, b_ref, *rest):
    chans, ring, pc, rows, piece, pieces, blk, width = dims
    if cross:
        cross_hbm, rest = rest[0], rest[1:]
    (
        pg_ref, wsum_ref, vec_ref,
        act_raw, cot_raw, X, Nn, Pm, LR, GX, Dall, Ow, RC, YS, YR, INV, S, SR, SB, SY,
        WA, GA, WS, VS, wt_ref, wb_ref, gain_ref, bias_ref,
        ld, ys, yr, cs, cr, fs, fr, rs, rr, os_, or_, qs, qr, ts, tr, us, ur, zs, zr, wbs, wbr, vs, vr,
    ) = rest[:51]
    if cross:
        BL, GY = rest[51:]
    me = lax.axis_index("rows")
    mine = lax.axis_index("chan")
    core = mine + 1 - 2 * (mine % 2)
    flipped = (mine + chans // 2) % chans
    far = core + 0
    far = (core + chans // 2) % chans
    row_first = me * rows
    place = ring_place(me, ring)
    right = ring_at((place + 1) % ring, ring)
    left = ring_at((place + ring - 1) % ring, ring)
    halves = 2
    owns = [(row_first + p * piece) // blk for p in range(pieces)]

    blocks = width // blk
    picks, paired = [], []
    for p in range(pieces):
        active = [contact_ref[owns[p], b] for b in range(blocks)]
        picks.append([(active[b] > 0) & (owns[p] != b) for b in range(blocks)])
        paired.append((sum(active[1:], active[0]) - 1).astype(jnp.float32))

    def second_of(p, read):
        out = read(0)
        for b in range(1, blocks):
            out = jnp.where(picks[p][b], read(b), out)
        return out

    loads = []
    cot_load = pltpu.make_async_copy(cot_hbm, cot_raw, ld.at[0])
    cot_load.start()
    act_load = pltpu.make_async_copy(act_hbm, act_raw, ld.at[1])
    act_load.start()
    if cross:
        cross_load = pltpu.make_async_copy(cross_hbm, BL, ld.at[2])
        cross_load.start()

    barrier = pltpu.get_barrier_semaphore()
    for hop in range(1, ring):
        pl.semaphore_signal(barrier, inc=1, device_id=((me + hop) % ring, mine), device_id_type=MESH)
    for hop in range(1, chans):
        pl.semaphore_signal(barrier, inc=1, device_id=(me, (mine + hop) % chans), device_id_type=MESH)
    pl.semaphore_wait(barrier, ring - 1 + chans - 1)

    def remote(src, dst, send, recv, r, c):
        return pltpu.make_async_remote_copy(
            src_ref=src, dst_ref=dst, send_sem=send, recv_sem=recv,
            device_id=(r, c), device_id_type=MESH,
        )

    for i, ref in enumerate((lg_ref, lv_ref, rg_ref, rv_ref)):
        wt_ref[i * pc : (i + 1) * pc, :] = ref[...]
    wb_ref[...] = jnp.transpose(wt_ref[...].astype(jnp.float32)).astype(jnp.bfloat16)
    square = (pc * chans, blk)
    gain_ref[...] = jnp.transpose(jnp.broadcast_to(g_ref[...], square))
    bias_ref[...] = jnp.transpose(jnp.broadcast_to(b_ref[...], square))

    act_load.wait()

    def turn(p):
        def gather_own(c, carry):
            own_col = pl.multiple_of(owns[p] * blk, blk)
            at = pl.ds(pl.multiple_of(c * rows + p * piece, piece), piece)
            span = pl.ds(p * piece, piece)
            LR[0, at, :] = act_raw[c, span, pl.ds(own_col, blk)].astype(jnp.float32)
            LR[1, at, :] = second_of(
                p, lambda b: act_raw[c, span, b * blk : (b + 1) * blk].astype(jnp.float32)
            )
            return carry

        lax.fori_loop(0, pc, gather_own, 0, unroll=4)

        def spread(k, carry):
            for hf in range(halves):
                X[hf, k, mine] = LR[hf, pl.ds(k, pc, stride=rows), :].astype(jnp.bfloat16)
            return carry

        lax.fori_loop(p * piece, (p + 1) * piece, spread, 0, unroll=4)

    def act_slab(p, c):
        return X.at[:, pl.ds(p * piece, piece), c]

    y_copies, c_copies, f_copies = [], [], []
    for p in range(pieces):
        turn(p)
        slab = act_slab(p, mine)
        y = remote(slab, slab, ys.at[p], yr.at[p], me, flipped)
        y.start()
        c = remote(slab, slab, cs.at[p], cr.at[p], me, core)
        c.start()
        y_copies.append(y)
        c_copies.append(c)

    cot_load.wait()

    def pick_cot(h, carry):
        for p in range(pieces):
            span = pl.ds(p * piece, piece)
            own_col = pl.multiple_of(owns[p] * blk, blk)
            at = pl.ds(pl.multiple_of(row_first + p * piece, piece), piece)
            Dall[h, at, :] = cot_raw[h, span, pl.ds(own_col, blk)]
            other = paired[p] * second_of(
                p, lambda b: cot_raw[h, span, b * blk : (b + 1) * blk].astype(jnp.float32)
            )
            Ow[h, pl.ds(rows + p * piece, piece), :] = other.astype(jnp.bfloat16)
        return carry

    def ring_copy(way, step, ch):
        if way == 0:
            unit, to = ring_at((place - (step - 1) + ring) % ring, ring), right
        else:
            unit, to = ring_at((place + (step - 1)) % ring, ring), left
        size = pc // CHUNKS
        view = Dall.at[pl.ds(ch * size, size), pl.ds(pl.multiple_of(unit * rows, rows), rows)]
        return remote(view, view, rs.at[way, step - 1, ch], rr.at[way, step - 1, ch], to, mine)

    top = ring // 2

    def ways_of(step, ch):
        if step < top:
            return [0, 1]
        return [ch % 2]

    def window_copy(way, p):
        to = (me + 1) % ring if way == 0 else (me + ring - 1) % ring
        src = Ow.at[:, pl.ds(rows + p * piece, piece)]
        dst = Ow.at[:, pl.ds((0 if way == 0 else 2 * rows) + p * piece, piece)]
        return remote(src, dst, os_.at[way, p], or_.at[way, p], to, mine)

    def first_own(d):
        return (d * rows) // blk

    def last_own(d):
        return (d * rows + rows - piece) // blk

    def sends_window(way, p):
        if way == 0:
            return (me < ring - 1) & (owns[p] == first_own(me + 1))
        return (me > 0) & (owns[p] == last_own(me - 1))

    def gets_window(way, p):
        if way == 0:
            return (me > 0) & (((me - 1) * rows + p * piece) // blk == first_own(me))
        return (me < ring - 1) & (((me + 1) * rows + p * piece) // blk == last_own(me))

    def run_pick():
        lax.fori_loop(0, pc, pick_cot, 0, unroll=2)

    run_pick()
    for way in (0, 1):
        for p in range(pieces):
            @pl.when(sends_window(way, p))
            def _(way=way, p=p):
                window_copy(way, p).start()
    for ch in range(CHUNKS):
        for way in (0, 1):
            ring_copy(way, 1, ch).start()

    def forward(step, ch):
        for way in (0, 1):
            if way in ways_of(step - 1, ch):
                ring_copy(way, step - 1, ch).wait_recv()
        if step <= top:
            for way in ways_of(step, ch):
                ring_copy(way, step, ch).start()

    inv_chan = 1.0 / (pc * chans)

    def ahead(p):
        def body(k, carry):
            normed = []
            for hf in range(halves):
                x = X[hf, k].reshape(pc * chans, blk).astype(jnp.float32)
                mean = jnp.sum(x, axis=0, keepdims=True) * inv_chan
                square = jnp.sum(x * x, axis=0, keepdims=True) * inv_chan
                inv = lax.rsqrt(square - mean * mean + EPS)
                standard = (x - mean) * inv
                INV[hf, pl.ds(k, 1), :] = inv
                n = (standard * gain_ref[...] + bias_ref[...]).astype(jnp.bfloat16)
                X[hf, k] = standard.astype(jnp.bfloat16).reshape(chans, pc, blk)
                Nn[hf, k] = n.reshape(chans, pc, blk)
                normed.append(n)
            projected = dot(wt_ref[...], jnp.concatenate(normed, axis=1))
            for hf in range(halves):
                part = projected[:, hf * blk : (hf + 1) * blk]
                ls = jax.nn.sigmoid(part[:pc])
                ll = part[pc : 2 * pc]
                rsig = jax.nn.sigmoid(part[2 * pc : 3 * pc])
                rl = part[3 * pc :]
                Pm[hf, k, 0:pc] = ls
                Pm[hf, k, pc : 2 * pc] = ll
                Pm[hf, k, 2 * pc : 3 * pc] = rsig
                Pm[hf, k, 3 * pc :] = rl
                lv, rv = ls * ll, rsig * rl
                if hf == 1:
                    lv, rv = lv * paired[p], rv * paired[p]
                LR[hf, pl.ds(k, pc, stride=rows), :] = lv
                LR[hf, pl.ds(pc * rows + k, pc, stride=rows), :] = rv
            return carry

        lax.fori_loop(p * piece, (p + 1) * piece, body, 0, unroll=2)

    def arrive(p):
        y_copies[p].wait_recv()
        slab = act_slab(p, flipped)
        f = remote(slab, slab, fs.at[p], fr.at[p], me, core)
        f.start()
        f_copies.append(f)
        c_copies[p].wait_recv()
        f.wait_recv()
        y_copies[p].wait_send()
        c_copies[p].wait_send()
        f.wait_send()

    arrive(0)
    ahead(0)
    forward(2, 0)
    forward(2, 1)
    if pieces > 1:
        arrive(1)
        ahead(1)
    forward(3, 0)
    for p in range(2, pieces):
        arrive(p)
        ahead(p)
    forward(3, 1)

    for way in (0, 1):
        for p in range(pieces):
            @pl.when(gets_window(way, p))
            def _(way=way, p=p):
                window_copy(way, p).wait_recv()
    for step in range(4, top + 1):
        forward(step, 0)
        forward(step, 1)
    if cross:
        cross_load.wait()

    def lr_rows(which, h, p):
        return pl.ds(pl.multiple_of((which * pc + h) * rows + p * piece, piece), piece)

    def near(h, carry):
        for p in range(pieces):
            own_at = pl.ds(pl.multiple_of(owns[p] * blk, blk), blk)
            win_at = pl.ds(pl.multiple_of(owns[p] * blk - row_first + rows, piece), blk)
            tl, tri = Dall[h, own_at, :], Ow[h, win_at, :]
            l0 = LR[0, lr_rows(0, h, p), :].astype(jnp.bfloat16)
            r0 = LR[0, lr_rows(1, h, p), :].astype(jnp.bfloat16)
            r1 = LR[1, lr_rows(1, h, p), :].astype(jnp.bfloat16)
            gl = dot_t(r0, tl) + dot_t(r1, tri)
            gr = dot(l0, jnp.concatenate([tl, tri], axis=1))
            at = pl.ds(pl.multiple_of(h * rows + p * piece, piece), piece)
            gr0 = gr[:, :blk]
            if cross:
                l1 = LR[1, lr_rows(0, h, p), :].astype(jnp.bfloat16)
                gr0 = gr0 + dot(l1, BL[h, p])
                GY[at, :] = dot_t(r0, BL[h, p])
            LR[0, lr_rows(0, h, p), :] = gl
            LR[0, lr_rows(1, h, p), :] = gr0
            GX[at, :] = gr[:, blk:]
        return carry

    def run_near():
        lax.fori_loop(0, pc, near, 0)

    run_near()

    def distant(h, carry):
        for p in range(pieces):
            br = second_of(p, lambda b: Dall[h, b * blk : (b + 1) * blk, :])
            l1 = LR[1, lr_rows(0, h, p), :].astype(jnp.bfloat16)
            r1 = LR[1, lr_rows(1, h, p), :].astype(jnp.bfloat16)
            at = pl.ds(pl.multiple_of(h * rows + p * piece, piece), piece)
            gl = dot_t(r1, br)
            if cross:
                gl = gl + GY[at, :]
            LR[1, lr_rows(0, h, p), :] = gl
            LR[1, lr_rows(1, h, p), :] = GX[at, :] + dot(l1, br)
        return carry

    def run_distant():
        lax.fori_loop(0, pc, distant, 0)

    WA[...] = jnp.zeros_like(WA)
    GA[...] = jnp.zeros_like(GA)

    def back(hf, p):
        def body(i, carry):
            grads, total = [], None
            for u in range(2):
                k = p * piece + 2 * i + u
                gl = LR[hf, pl.ds(k, pc, stride=rows), :]
                gr = LR[hf, pl.ds(pc * rows + k, pc, stride=rows), :]
                if hf == 1:
                    gl, gr = gl * paired[p], gr * paired[p]
                ls, ll = Pm[hf, k, 0:pc], Pm[hf, k, pc : 2 * pc]
                rsig, rl = Pm[hf, k, 2 * pc : 3 * pc], Pm[hf, k, 3 * pc :]
                a, b = gl * ls, gr * rsig
                g = jnp.concatenate([a * ll * (1.0 - ls), a, b * rl * (1.0 - rsig), b], axis=0)
                total = g if total is None else total + g
                grads.append(g.astype(jnp.bfloat16))
            GA[...] += total
            pair = jnp.concatenate(grads, axis=1)
            partial = dot(wb_ref[...], pair)
            both = []
            for u in range(2):
                k = p * piece + 2 * i + u
                n = partial[:, u * blk : (u + 1) * blk]
                st = X[hf, k].reshape(pc * chans, blk)
                scaled = n * gain_ref[...]
                S[hf, 0, pl.ds(k, 1), :] = jnp.sum(scaled, axis=0, keepdims=True)
                S[hf, 1, pl.ds(k, 1), :] = jnp.sum(scaled * st.astype(jnp.float32), axis=0, keepdims=True)
                both.append(jnp.concatenate([Nn[hf, k].reshape(pc * chans, blk), st], axis=0))
                Nn[hf, k] = n.astype(jnp.bfloat16).reshape(chans, pc, blk)
            WA[...] += dot_t(pair, jnp.concatenate(both, axis=1))
            return carry

        lax.fori_loop(0, piece // 2, body, 0)

    def span_of(p):
        return pl.ds(p * piece, piece)

    def core_copies(hf, p):
        at = span_of(p)
        return [
            remote(Nn.at[hf, at, core], RC.at[0, hf, at], qs.at[hf, p, 0], qr.at[hf, p, 0], me, core),
            remote(Nn.at[hf, at, far], RC.at[1, hf, at], qs.at[hf, p, 1], qr.at[hf, p, 1], me, core),
            remote(S.at[hf, :, at], SR.at[hf, :, at], ts.at[hf, p], tr.at[hf, p], me, core),
        ]

    def y_back(hf, p):
        at = span_of(p)
        return [
            remote(YS.at[hf, at], YR.at[hf, at], us.at[hf, p], ur.at[hf, p], me, flipped),
            remote(SB.at[hf, :, at], SY.at[hf, :, at], zs.at[hf, p], zr.at[hf, p], me, flipped),
        ]

    def combine(hf, p):
        for c in core_copies(hf, p):
            c.wait_recv()
        at = span_of(p)
        YS[hf, at] = (
            Nn[hf, at, flipped].astype(jnp.float32) + RC[1, hf, at].astype(jnp.float32)
        ).astype(jnp.bfloat16)
        total = S[hf, :, at, :] + SR[hf, :, at, :]
        SR[hf, :, at, :] = total
        SB[hf, :, at, :] = total.astype(jnp.bfloat16)
        for c in y_back(hf, p):
            c.start()

    scale = 1.0 / (pc * chans)

    def finish(hf, p):
        for c in y_back(hf, p):
            c.wait_recv()
        at = span_of(p)
        SR[hf, :, at, :] = (SR[hf, :, at, :] + SY[hf, :, at, :].astype(jnp.float32)) * scale
        gain = gain_ref[pl.ds(pl.multiple_of(mine * pc, pc), pc), :]

        def body(k, carry):
            n = (
                Nn[hf, k, mine].astype(jnp.float32)
                + RC[0, hf, k].astype(jnp.float32)
                + YR[hf, k].astype(jnp.float32)
            )
            st = X[hf, k, mine].astype(jnp.float32)
            s0 = SR[hf, 0, pl.ds(k, 1), :]
            s1 = SR[hf, 1, pl.ds(k, 1), :]
            out = (n * gain - s0 - st * s1) * INV[hf, pl.ds(k, 1), :]
            LR[hf, pl.ds(k, pc, stride=rows), :] = out
            return carry

        lax.fori_loop(p * piece, (p + 1) * piece, body, 0, unroll=4)

        def put(c, carry):
            rows_at = pl.ds(pl.multiple_of(c * rows + p * piece, piece), piece)
            pg_ref[hf, c, at, :] = LR[hf, rows_at, :].astype(jnp.bfloat16)
            return carry

        lax.fori_loop(0, pc, put, 0, unroll=4)

    items = [(hf, p) for hf in range(halves) for p in range(pieces)]
    pending = None
    for hf, p in items:
        if hf == 1 and p == 0:
            forward(top + 1, 0)
            forward(top + 1, 1)
            run_distant()
        back(hf, p)
        for c in core_copies(hf, p):
            c.start()
        if pending is not None:
            combine(*pending)
        pending = (hf, p)
    combine(*pending)

    allc = pc * chans
    wide = wt_ref[...].astype(jnp.float32)
    gain_term = jnp.sum(wide * WA[:, allc:], axis=0, keepdims=True)
    bias_term = jnp.sum(wide * jnp.sum(GA[...], axis=1, keepdims=True), axis=0, keepdims=True)
    sub = lax.broadcasted_iota(jnp.int32, (8, allc), 0)
    WS[me, : 4 * pc, :] = WA[:, :allc]
    WS[me, 4 * pc :, :] = jnp.where(sub == 0, gain_term, jnp.where(sub == 1, bias_term, 0.0))

    def wide_copy(hop):
        return remote(
            WS.at[me], WS.at[me], wbs.at[hop - 1], wbr.at[hop - 1], (me + hop) % ring, mine
        )

    for hop in range(1, ring):
        wide_copy(hop).start()

    for p in range(pieces):
        finish(0, p)

    for hop in range(1, ring):
        wide_copy(hop).wait_recv()
    summed = WS[0]
    for d in range(1, ring):
        summed = summed + WS[d]
    summed = summed * (1.0 / width)
    wsum_ref[...] = summed[: 4 * pc]
    VS[mine] = summed[4 * pc :]

    def vec_copy(hop):
        return remote(VS.at[mine], VS.at[mine], vs.at[hop - 1], vr.at[hop - 1], me, (mine + hop) % chans)

    for hop in range(1, chans):
        vec_copy(hop).start()
    for p in range(pieces):
        finish(1, p)
    for hop in range(1, chans):
        vec_copy(hop).wait_recv()
    total = VS[0]
    for d in range(1, chans):
        total = total + VS[d]
    vec_ref[...] = total

    for way in (0, 1):
        for p in range(pieces):
            @pl.when(sends_window(way, p))
            def _(way=way, p=p):
                window_copy(way, p).wait_send()
    for step in range(1, top + 1):
        for ch in range(CHUNKS):
            for way in ways_of(step, ch):
                ring_copy(way, step, ch).wait_send()
    for hf, p in items:
        for c in core_copies(hf, p) + y_back(hf, p):
            c.wait_send()
    for hop in range(1, ring):
        wide_copy(hop).wait_send()
    for hop in range(1, chans):
        vec_copy(hop).wait_send()


def call_mega(cross, dims, contact, act, cot, gates, gain, bias, *extra):
    chans, ring, pc, rows, piece, pieces, blk, width = dims
    allc = pc * chans
    bf, f32 = jnp.bfloat16, jnp.float32
    V, D = pltpu.VMEM, pltpu.SemaphoreType.DMA
    top = ring // 2
    scratch = [
        V((pc, rows, width), bf), V((pc, rows, width), bf),
        V((2, rows, chans, pc, blk), bf), V((2, rows, chans, pc, blk), bf),
        V((2, rows, 4 * pc, blk), f32), V((2, 2 * pc * rows, blk), f32), V((pc * rows, blk), f32),
        V((pc, ring * rows, blk), bf), V((pc, 3 * rows, blk), bf),
        V((2, 2, rows, pc, blk), bf), V((2, rows, pc, blk), bf), V((2, rows, pc, blk), bf),
        V((2, rows, blk), f32), V((2, 2, rows, blk), f32), V((2, 2, rows, blk), f32),
        V((2, 2, rows, blk), bf), V((2, 2, rows, blk), bf),
        V((4 * pc, 2 * allc), f32), V((4 * pc, blk), f32),
        V((ring, 4 * pc + 8, allc), f32), V((chans, 8, allc), f32),
        V((4 * pc, allc), bf), V((allc, 4 * pc), bf), V((allc, blk), f32), V((allc, blk), f32),
        D((3,)), D((pieces,)), D((pieces,)), D((pieces,)), D((pieces,)), D((pieces,)), D((pieces,)),
        D((2, top, CHUNKS)), D((2, top, CHUNKS)), D((2, pieces)), D((2, pieces)),
        D((2, pieces, 2)), D((2, pieces, 2)), D((2, pieces)), D((2, pieces)),
        D((2, pieces)), D((2, pieces)), D((2, pieces)), D((2, pieces)),
        D((ring - 1,)), D((ring - 1,)), D((chans - 1,)), D((chans - 1,)),
    ]
    if cross:
        scratch += [V((pc, pieces, blk, blk), bf), V((pc * rows, blk), f32)]
    vmem = pl.BlockSpec(memory_space=pltpu.VMEM)
    hbm = pl.BlockSpec(memory_space=pl.ANY)
    return pl.pallas_call(
        functools.partial(mega, cross, dims),
        out_shape=(
            jax.ShapeDtypeStruct((2, pc, rows, blk), bf),
            jax.ShapeDtypeStruct((4 * pc, allc), f32),
            jax.ShapeDtypeStruct((8, allc), f32),
        ),
        in_specs=[pl.BlockSpec(memory_space=pltpu.SMEM), hbm, hbm] + [vmem] * 6
        + [hbm] * len(extra),
        out_specs=(vmem, vmem, vmem),
        scratch_shapes=scratch,
        compiler_params=pltpu.CompilerParams(
            collective_id=2 if cross else 1, has_side_effects=True, vmem_limit_bytes=VMEM_BYTES
        ),
        name="triangle_cross" if cross else "triangle",
    )(contact, act, cot, *gates, gain, bias, *extra)


def expand(dims, contact_ref, pg_ref, wsum_ref, vec_ref, out_ref, g_ref, b_ref, *w_refs):
    chans, ring, pc, rows, piece, pieces, blk, width = dims
    row_first = lax.axis_index("rows") * rows
    for p in range(pieces):
        own = (row_first + p * piece) // blk
        at = pl.ds(p * piece, piece)
        near, far = pg_ref[0, :, at, :], pg_ref[1, :, at, :]
        none = jnp.zeros_like(near)
        for b in range(width // blk):
            held = jnp.where(contact_ref[own, b] > 0, far, none)
            out_ref[:, at, b * blk : (b + 1) * blk] = jnp.where(own == b, near, held)

    @pl.when(pl.program_id(0) == 0)
    def _():
        allc = pc * chans
        mine = lax.axis_index("chan")
        vec = pltpu.roll(vec_ref[...], (allc - mine * pc) % allc, 1)
        g_ref[...] = vec[0:1, :pc]
        b_ref[...] = vec[1:2, :pc]
        for i, ref in enumerate(w_refs):
            ref[...] = wsum_ref[i * pc : (i + 1) * pc, :]


def call_expand(dims, contact, pg, wsum, vec, steps=4):
    chans, ring, pc, rows, piece, pieces, blk, width = dims
    allc = pc * chans
    f32 = jnp.float32

    def whole(shape):
        return pl.BlockSpec(shape, lambda i: (0,) * len(shape))

    return pl.pallas_call(
        functools.partial(expand, dims),
        grid=(steps,),
        out_shape=(
            jax.ShapeDtypeStruct((pc, rows, width), pg.dtype),
            jax.ShapeDtypeStruct((1, pc), f32),
            jax.ShapeDtypeStruct((1, pc), f32),
        )
        + (jax.ShapeDtypeStruct((pc, allc), f32),) * 4,
        in_specs=[
            pl.BlockSpec(memory_space=pltpu.SMEM),
            pl.BlockSpec((2, pc // steps, rows, blk), lambda i: (0, i, 0, 0)),
            whole((4 * pc, allc)),
            whole((8, allc)),
        ],
        out_specs=(
            pl.BlockSpec((pc // steps, rows, width), lambda i: (i, 0, 0)),
            whole((1, pc)),
            whole((1, pc)),
        )
        + (whole((pc, allc)),) * 4,
        name="expand",
    )(contact, pg, wsum, vec)


def everywhere(x, rows, width, row_first):
    ring = lax.axis_size("rows")
    order = ring_order(ring)
    place = [order.index(d) for d in range(ring)]
    order_table = jnp.array(order, jnp.int32)
    my_place = jnp.array(place, jnp.int32)[lax.axis_index("rows")]
    right_perm = [(order[i], order[(i + 1) % ring]) for i in range(ring)]
    left_perm = [(order[(i + 1) % ring], order[i]) for i in range(ring)]
    half, top = x.shape[0] // 2, ring // 2
    out = jnp.zeros((x.shape[0], width, x.shape[2]), x.dtype)
    out = lax.dynamic_update_slice(out, x, (0, row_first, 0))
    going_right, going_left = x, x
    for step in range(1, top + 1):
        last = step == top and ring % 2 == 0
        if last:
            going_right, going_left = going_right[:half], going_left[half:]
        going_right = lax.ppermute(going_right, "rows", right_perm)
        going_left = lax.ppermute(going_left, "rows", left_perm)
        from_left = order_table[(my_place - step + ring) % ring] * rows
        from_right = order_table[(my_place + step) % ring] * rows
        out = lax.dynamic_update_slice(out, going_right, (0, from_left, 0))
        out = lax.dynamic_update_slice(out, going_left, (half if last else 0, from_right, 0))
    return out


def fused(
    pair_act, pair_cot, contact, ln_gain, ln_bias, left_gate, left_value, right_gate, right_value
):
    pc, rows, width = pair_act.shape
    blocks = contact.shape[0]
    blk = width // blocks
    chans, ring = lax.axis_size("chan"), lax.axis_size("rows")
    piece = math.gcd(rows, blk)
    pieces = rows // piece
    dims = (chans, ring, pc, rows, piece, pieces, blk, width)
    row_first = lax.axis_index("rows") * rows
    mutual = jnp.sum(contact * contact.T) > blocks
    gates = (left_gate.T, left_value.T, right_gate.T, right_value.T)
    args = (contact, pair_act, pair_cot, gates, ln_gain[None], ln_bias[None])

    def simple(args):
        return call_mega(False, dims, *args)

    def crossed(args):
        cot = args[2]
        numbers = jnp.arange(blocks, dtype=jnp.int32)
        paired = jnp.sum(contact, axis=1) > 1
        other = jnp.where(paired, jnp.sum(contact * numbers[None, :], axis=1) - numbers, numbers)
        owns = [(row_first + p * piece) // blk for p in range(pieces)]
        seconds = [other[own] for own in owns]
        part = jnp.concatenate(
            [
                lax.dynamic_slice(cot, (0, p * piece, seconds[p] * blk), (pc, piece, blk))
                for p in range(pieces)
            ],
            axis=1,
        )
        every = everywhere(part, rows, width, row_first)
        corners = []
        for p in range(pieces):
            own, second = owns[p], seconds[p]
            good = (second != own) & (other[second] == own)
            here = lax.dynamic_slice(every, (0, second * blk, 0), (pc, blk, blk))
            corners.append(jnp.where(good, here, jnp.zeros((), here.dtype)))
        return call_mega(True, dims, *args, jnp.stack(corners, axis=1))

    held = lax.cond(mutual, crossed, simple, args)
    out = call_expand(dims, contact, *held)
    return (out[0], out[1][0], out[2][0]) + tuple(w.T for w in out[3:])


def local(*arrays):
    pc, rows, width = arrays[0].shape
    blk = width // arrays[2].shape[0]
    piece = math.gcd(rows, blk)
    chans, ring = lax.axis_size("chan"), lax.axis_size("rows")
    fits = (
        piece % 16 == 0 and rows // piece == 3 and blk == pc * chans == 4 * pc and ring == 8
    )
    return fused(*arrays) if fits else plain(*arrays)


def solution(mesh):
    in_specs = (
        P("chan", "rows", None),
        P("chan", "rows", None),
        P(),
        P(),
        P(),
        P(None, "chan"),
        P(None, "chan"),
        P(None, "chan"),
        P(None, "chan"),
    )
    out_specs = (
        P("chan", "rows", None),
        P("chan"),
        P("chan"),
        P(None, "chan"),
        P(None, "chan"),
        P(None, "chan"),
        P(None, "chan"),
    )
    return jax.shard_map(local, mesh=mesh, in_specs=in_specs, out_specs=out_specs, check_vma=False)
```

```python
import functools
import math

import jax
import jax.numpy as jnp
from jax import lax
from jax.experimental import pallas as pl
from jax.experimental.pallas import tpu as pltpu
from jax.sharding import PartitionSpec as P

EPS = 1e-05


def ring_order(count):
    return list(range(0, count, 2)) + list(range(1, count, 2))[::-1]


def flip(x, axis, bit):
    count = lax.axis_size(axis)
    return lax.ppermute(x, axis, [(d, d ^ bit) for d in range(count)])


def bits_down(count):
    bits = [1 << b for b in range(count.bit_length() - 1)]
    return bits[::-1]


def plain(
    pair_act, pair_cot, contact, ln_gain, ln_bias, left_gate, left_value, right_gate, right_value
):
    part_chan, rows_here, width = pair_act.shape
    part_hid = pair_cot.shape[0]
    blocks = contact.shape[0]
    block_len = width // blocks
    chans = lax.axis_size("chan")
    ring = lax.axis_size("rows")
    all_chan = part_chan * chans
    mine = lax.axis_index("chan")
    row_first = lax.axis_index("rows") * rows_here
    piece = math.gcd(rows_here, block_len)
    pieces = rows_here // piece

    numbers = jnp.arange(blocks, dtype=jnp.int32)
    other = jnp.sum(contact * numbers[None, :], axis=1) - numbers
    paired = jnp.sum(contact, axis=1) > 1
    row_block = (row_first + jnp.arange(rows_here, dtype=jnp.int32)) // block_len
    at_own = row_block[:, None] == numbers[None, :]
    row_other = jnp.sum(jnp.where(at_own, other[None, :], 0), axis=1)
    row_paired = jnp.sum(jnp.where(at_own, paired[None, :].astype(jnp.int32), 0), axis=1) > 0
    at_other = (row_other[:, None] == numbers[None, :]) & row_paired[:, None]
    weight = jnp.concatenate(
        [
            jnp.ones((rows_here, block_len), jnp.float32),
            jnp.broadcast_to(
                row_paired.astype(jnp.float32)[:, None], (rows_here, block_len)
            ),
        ],
        axis=1,
    )

    def compact(x):
        def pick(at):
            out = jnp.zeros((x.shape[0], rows_here, block_len), x.dtype)
            for b in range(blocks):
                here = x[:, :, b * block_len : (b + 1) * block_len]
                out = jnp.where(at[:, b][None, :, None], here, out)
            return out

        return jnp.concatenate([pick(at_own), pick(at_other)], axis=2)

    cot = compact(pair_cot)
    own_cot, other_cot = cot[:, :, :block_len], cot[:, :, block_len:]
    order = ring_order(ring)
    place = [order.index(d) for d in range(ring)]
    order_table = jnp.array(order, jnp.int32)
    my_place = jnp.array(place, jnp.int32)[lax.axis_index("rows")]
    right_perm = [(order[i], order[(i + 1) % ring]) for i in range(ring)]
    left_perm = [(order[(i + 1) % ring], order[i]) for i in range(ring)]
    act = compact(pair_act)

    def go_round(x):
        half = x.shape[0] // 2
        top = ring // 2
        arrived = []
        going_right, going_left = x, x
        for step in range(1, top + 1):
            last = step == top and ring % 2 == 0
            if last:
                going_right, going_left = going_right[:half], going_left[half:]
            going_right = lax.ppermute(going_right, "rows", right_perm)
            going_left = lax.ppermute(going_left, "rows", left_perm)
            from_left = order_table[(my_place - step + ring) % ring] * rows_here
            from_right = order_table[(my_place + step) % ring] * rows_here
            arrived.append((going_right, 0, from_left))
            arrived.append((going_left, half if last else 0, from_right))
        here, _ = lax.optimization_barrier((x, arrived[0][0]))
        out = jnp.zeros((x.shape[0], width, x.shape[2]), x.dtype)
        out = lax.dynamic_update_slice(out, here, (0, row_first, 0))
        for block, first, at in arrived:
            out = lax.dynamic_update_slice(out, block, (first, at, 0))
        return out

    gathered = go_round(own_cot)
    reach = -(-(block_len - piece) // rows_here)
    window = [other_cot]
    for hop in range(1, min(reach, ring - 1) + 1):
        up = [(d, d + hop) for d in range(ring - hop)]
        down = [(d + hop, d) for d in range(ring - hop)]
        window = (
            [lax.ppermute(other_cot, "rows", up)]
            + window
            + [lax.ppermute(other_cot, "rows", down)]
        )
    window_first = row_first - (len(window) // 2) * rows_here
    window = jnp.concatenate(window, axis=1)
    owns = [(row_first + p * piece) // block_len for p in range(pieces)]
    seconds = [other[own] for own in owns]
    mutual_row = paired & paired[other] & (other[other] == numbers)

    def crossed(x):
        everywhere = go_round(x)
        return [
            jnp.where(
                mutual_row[own],
                lax.dynamic_slice(
                    everywhere, (0, second * block_len, 0), (part_hid, block_len, block_len)
                ),
                jnp.zeros((), x.dtype),
            )
            for own, second in zip(owns, seconds)
        ]

    def uncrossed(x):
        return [jnp.zeros((part_hid, block_len, block_len), x.dtype) for _ in owns]

    cross = lax.cond(jnp.any(mutual_row), crossed, uncrossed, other_cot)

    parts, offsets = [act], [0]
    for bit in bits_down(chans):
        parts = parts + [flip(x, "chan", bit) for x in parts]
        offsets = offsets + [o + bit for o in offsets]
    full_act = jnp.concatenate(parts, axis=0).astype(jnp.float32)
    partner = jnp.array(offsets, jnp.int32) ^ mine

    def by_partner(x):
        return x.reshape((chans, part_chan) + x.shape[1:])[partner].reshape(x.shape)

    slot_of = [offsets.index(o) for o in range(chans)]
    back_order = jnp.array(slot_of, jnp.int32)[jnp.arange(chans, dtype=jnp.int32) ^ mine]

    def by_channel(x):
        return x.reshape((chans, part_chan) + x.shape[1:])[back_order].reshape(x.shape)

    gain = by_partner(ln_gain)
    bias = by_partner(ln_bias)
    w_stacked = by_partner(
        jnp.concatenate([left_gate, left_value, right_gate, right_value], axis=1)
    )

    mean = jnp.mean(full_act, axis=0)
    inv_std = lax.rsqrt(jnp.mean(full_act * full_act, axis=0) - mean * mean + EPS)
    standard = (full_act - mean) * inv_std
    normed = (standard * gain[:, None, None] + bias[:, None, None]).astype(jnp.bfloat16)
    standard_near = standard.astype(jnp.bfloat16)
    projected = jnp.einsum("ch,ckn->hkn", w_stacked, normed, preferred_element_type=jnp.float32)
    left_logit, left_linear, right_logit, right_linear = jnp.split(projected, 4, axis=0)
    left_sigmoid = jax.nn.sigmoid(left_logit)
    right_sigmoid = jax.nn.sigmoid(right_logit)
    left = (weight * left_sigmoid * left_linear).astype(jnp.bfloat16)
    right = (weight * right_sigmoid * right_linear).astype(jnp.bfloat16)

    corners = []
    for own, second, back_cross in zip(owns, seconds, cross):
        size = (part_hid, block_len, block_len)
        top = jnp.concatenate(
            [
                lax.dynamic_slice(gathered, (0, own * block_len, 0), size),
                lax.dynamic_slice(window, (0, own * block_len - window_first, 0), size),
            ],
            axis=2,
        )
        low = jnp.concatenate(
            [back_cross, lax.dynamic_slice(gathered, (0, second * block_len, 0), size)], axis=2
        )
        corners.append(jnp.concatenate([top, low], axis=1))
    corner = jnp.stack(corners, axis=1)

    def cut(x):
        return x.reshape(part_hid, pieces, piece, 2 * block_len)

    grad_left = jnp.einsum(
        "hpkj,hpij->hpki", cut(right), corner, preferred_element_type=jnp.float32
    ).reshape(left.shape)
    grad_right = jnp.einsum(
        "hpki,hpij->hpkj", cut(left), corner, preferred_element_type=jnp.float32
    ).reshape(left.shape)
    keep_left = grad_left * weight
    keep_right = grad_right * weight
    grads = jnp.concatenate(
        [
            (keep_left * left_linear * left_sigmoid * (1.0 - left_sigmoid)).astype(jnp.bfloat16),
            (keep_left * left_sigmoid).astype(jnp.bfloat16),
            (keep_right * right_linear * right_sigmoid * (1.0 - right_sigmoid)).astype(
                jnp.bfloat16
            ),
            (keep_right * right_sigmoid).astype(jnp.bfloat16),
        ],
        axis=0,
    )

    def back(rows):
        return jnp.einsum("ch,hkn->ckn", rows, grads, preferred_element_type=jnp.float32)

    w_parts = {o: w_stacked[i * part_chan : (i + 1) * part_chan] for i, o in enumerate(offsets)}
    partial = {o: back(w_parts[o]) for o in offsets}
    first_sum = jnp.zeros(mean.shape, jnp.float32)
    second_sum = jnp.zeros(mean.shape, jnp.float32)
    for i, o in enumerate(offsets):
        span = slice(i * part_chan, (i + 1) * part_chan)
        scaled = partial[o] * gain[span][:, None, None]
        first_sum = first_sum + jnp.sum(scaled, axis=0)
        second_sum = second_sum + jnp.sum(scaled * standard[span], axis=0)
    sums = jnp.stack([first_sum, second_sum])
    late_grads = grads
    for bit in bits_down(chans)[::-1]:
        leaving = {o: partial[o].astype(jnp.bfloat16) for o in partial if o & bit}
        received = {o - bit: flip(x, "chan", bit) for o, x in leaving.items()}
        late_grads, _ = lax.optimization_barrier((late_grads, tuple(leaving.values())))
        partial = {o: partial[o] + x.astype(jnp.float32) for o, x in received.items()}
        sums = sums + flip(sums, "chan", bit)
    normed_grad = partial[0]
    scaled = normed_grad * gain[:part_chan][:, None, None]
    pair_grad = (
        (scaled - sums[0] / all_chan - standard[:part_chan] * (sums[1] / all_chan)) * inv_std
    ).astype(jnp.bfloat16)
    near, far = pair_grad[:, :, :block_len], pair_grad[:, :, block_len:]
    none = jnp.zeros((), pair_grad.dtype)
    pair_grad = jnp.concatenate(
        [
            jnp.where(
                at_own[:, b][None, :, None],
                near,
                jnp.where(at_other[:, b][None, :, None], far, none),
            )
            for b in range(blocks)
        ],
        axis=2,
    )

    weight_total = jnp.einsum("ckn,hkn->ch", normed, late_grads, preferred_element_type=jnp.float32)
    moment = jnp.einsum("ckn,hkn->ch", standard_near, late_grads, preferred_element_type=jnp.float32)
    wide = w_stacked.astype(jnp.float32)
    gain_terms = jnp.sum(wide * moment, axis=1)
    bias_terms = jnp.sum(wide * jnp.sum(late_grads.astype(jnp.float32), axis=(1, 2))[None, :], axis=1)
    vectors = by_channel(jnp.stack([gain_terms, bias_terms], axis=1))
    for bit in bits_down(chans):
        vectors = vectors + flip(vectors, "chan", bit)
    vectors = lax.dynamic_slice_in_dim(vectors, mine * part_chan, part_chan, 0)
    for bit in bits_down(ring):
        vectors = vectors + flip(vectors, "rows", bit)
        weight_total = weight_total + flip(weight_total, "rows", bit)
    factor = 1.0 / width
    weight_total = by_channel(weight_total) * factor
    vectors = vectors * factor
    return (pair_grad, vectors[:, 0], vectors[:, 1]) + tuple(jnp.split(weight_total, 4, axis=1))


MESH = pl.DeviceIdType.MESH
VMEM_BYTES = 66 << 20
CHUNKS = 4
LAST_LEFT = 1
UNROLL = 4


def dot(a, b):
    return lax.dot_general(a, b, (((1,), (0,)), ((), ())), preferred_element_type=jnp.float32)


def dot_t(a, b):
    return lax.dot_general(a, b, (((1,), (1,)), ((), ())), preferred_element_type=jnp.float32)


def ring_at(place, ring):
    late = place // (ring // 2)
    return (1 - late) * 2 * place + late * (2 * (ring - 1 - place) + 1)


def ring_place(d, ring):
    return (1 - d % 2) * (d // 2) + (d % 2) * (ring - 1 - d // 2)


def mega(cross, dims, contact_ref, act_hbm, cot_hbm, lg_ref, lv_ref, rg_ref, rv_ref, g_ref, b_ref, *rest):
    chans, ring, pc, rows, piece, pieces, blk, width = dims
    if cross:
        cross_hbm, rest = rest[0], rest[1:]
    (
        pg_ref, wsum_ref, vec_ref,
        act_raw, cot_raw, X, Nn, Pm, LR, GX, Dall, Ow, RC, YS, YR, INV, S, SR, SB, SY,
        WA, GA, WS, VS, wt_ref, wb_ref, gain_ref, bias_ref,
        ld, ch_s, ys, yr, cs, cr, fs, fr, rs, rr, os_, or_, qs, qr, ts, tr, us, ur, zs, zr, wbs, wbr, vs, vr,
    ) = rest[:52]
    if cross:
        BL, GY = rest[52:]
    me = lax.axis_index("rows")
    mine = lax.axis_index("chan")
    core = mine + 1 - 2 * (mine % 2)
    flipped = (mine + chans // 2) % chans
    far = core + 0
    far = (core + chans // 2) % chans
    row_first = me * rows
    place = ring_place(me, ring)
    right = ring_at((place + 1) % ring, ring)
    left = ring_at((place + ring - 1) % ring, ring)
    halves = 2
    owns = [(row_first + p * piece) // blk for p in range(pieces)]

    blocks = width // blk
    picks, paired = [], []
    for p in range(pieces):
        active = [contact_ref[owns[p], b] for b in range(blocks)]
        picks.append([(active[b] > 0) & (owns[p] != b) for b in range(blocks)])
        paired.append((sum(active[1:], active[0]) - 1).astype(jnp.float32))

    def second_of(p, read):
        out = read(0)
        for b in range(1, blocks):
            out = jnp.where(picks[p][b], read(b), out)
        return out

    loads = []
    cot_load = pltpu.make_async_copy(cot_hbm, cot_raw, ld.at[0])
    cot_load.start()
    act_load = pltpu.make_async_copy(act_hbm, act_raw, ld.at[1])
    act_load.start()
    if cross:
        cross_load = pltpu.make_async_copy(cross_hbm, BL, ld.at[2])
        cross_load.start()

    barrier = pltpu.get_barrier_semaphore()
    for hop in range(1, ring):
        pl.semaphore_signal(barrier, inc=1, device_id=((me + hop) % ring, mine), device_id_type=MESH)
    for hop in range(1, chans):
        pl.semaphore_signal(barrier, inc=1, device_id=(me, (mine + hop) % chans), device_id_type=MESH)
    pl.semaphore_wait(barrier, ring - 1 + chans - 1)

    def remote(src, dst, send, recv, r, c):
        return pltpu.make_async_remote_copy(
            src_ref=src, dst_ref=dst, send_sem=send, recv_sem=recv,
            device_id=(r, c), device_id_type=MESH,
        )

    cot_load.wait()

    def pick_cot(h, carry):
        for p in range(pieces):
            span = pl.ds(p * piece, piece)
            own_col = pl.multiple_of(owns[p] * blk, blk)
            at = pl.ds(pl.multiple_of(row_first + p * piece, piece), piece)
            Dall[h, at, :] = cot_raw[h, span, pl.ds(own_col, blk)]
            other = paired[p] * second_of(
                p, lambda b: cot_raw[h, span, b * blk : (b + 1) * blk].astype(jnp.float32)
            )
            Ow[h, pl.ds(rows + p * piece, piece), :] = other.astype(jnp.bfloat16)
        return carry

    def ring_copy(way, step, ch):
        if way == 0:
            unit, to = ring_at((place - (step - 1) + ring) % ring, ring), right
        else:
            unit, to = ring_at((place + (step - 1)) % ring, ring), left
        size = pc // CHUNKS
        view = Dall.at[pl.ds(ch * size, size), pl.ds(pl.multiple_of(unit * rows, rows), rows)]
        return remote(view, view, rs.at[way, step - 1, ch], rr.at[way, step - 1, ch], to, mine)

    top = ring // 2

    def ways_of(step, ch):
        if step < top:
            return [0, 1]
        return [1] if ch >= CHUNKS - LAST_LEFT else [0]

    def pair_of(d):
        return d + 1 - 2 * (d % 2)

    def has_chord(d):
        return (d // 2 > 0) & (d // 2 < ring // 2 - 1)

    def chord_way(d):
        return (d % 2 + d // (ring // 2)) % 2

    def by_chord(d, way, step):
        if step != top - 1:
            return None
        return has_chord(d) & (chord_way(d) == way)

    def chord_copy(way, ch):
        size = pc // CHUNKS
        view = Dall.at[pl.ds(ch * size, size), pl.ds(pl.multiple_of(me * rows, rows), rows)]
        return remote(view, view, ch_s.at[ch], rr.at[way, top - 2, ch], pair_of(me), mine)

    def chord_sends(way):
        return has_chord(me) & (chord_way(pair_of(me)) == way)

    def unless(condition, act):
        if condition is None:
            act()
        else:
            pl.when(jnp.logical_not(condition))(act)

    def ring_start(way, step, ch):
        unless(
            by_chord(right if way == 0 else left, way, step),
            lambda: ring_copy(way, step, ch).start(),
        )

    def ring_sent(way, step, ch):
        unless(
            by_chord(right if way == 0 else left, way, step),
            lambda: ring_copy(way, step, ch).wait_send(),
        )

    def window_copy(way, p):
        to = (me + 1) % ring if way == 0 else (me + ring - 1) % ring
        src = Ow.at[:, pl.ds(rows + p * piece, piece)]
        dst = Ow.at[:, pl.ds((0 if way == 0 else 2 * rows) + p * piece, piece)]
        return remote(src, dst, os_.at[way, p], or_.at[way, p], to, mine)

    def first_own(d):
        return (d * rows) // blk

    def last_own(d):
        return (d * rows + rows - piece) // blk

    def sends_window(way, p):
        if way == 0:
            return (me < ring - 1) & (owns[p] == first_own(me + 1))
        return (me > 0) & (owns[p] == last_own(me - 1))

    def gets_window(way, p):
        if way == 0:
            return (me > 0) & (((me - 1) * rows + p * piece) // blk == first_own(me))
        return (me < ring - 1) & (((me + 1) * rows + p * piece) // blk == last_own(me))

    def run_pick():
        lax.fori_loop(0, pc, pick_cot, 0, unroll=2)

    run_pick()
    for ch in range(CHUNKS):
        for way in (0, 1):
            ring_copy(way, 1, ch).start()
    for way in (0, 1):
        @pl.when(chord_sends(way))
        def _(way=way):
            for ch in range(CHUNKS):
                chord_copy(way, ch).start()
    for way in (0, 1):
        for p in range(pieces):
            @pl.when(sends_window(way, p))
            def _(way=way, p=p):
                window_copy(way, p).start()

    def forward(step, way, chunks=range(CHUNKS)):
        for ch in chunks:
            if way in ways_of(step - 1, ch):
                unless(
                    by_chord(me, way, step - 1),
                    lambda: ring_copy(way, step - 1, ch).wait_recv(),
                )
            if step <= top and way in ways_of(step, ch):
                ring_start(way, step, ch)

    for i, ref in enumerate((lg_ref, lv_ref, rg_ref, rv_ref)):
        wt_ref[i * pc : (i + 1) * pc, :] = ref[...]
    wb_ref[...] = jnp.transpose(wt_ref[...].astype(jnp.float32)).astype(jnp.bfloat16)
    square = (pc * chans, blk)
    gain_ref[...] = jnp.transpose(jnp.broadcast_to(g_ref[...], square))
    bias_ref[...] = jnp.transpose(jnp.broadcast_to(b_ref[...], square))

    act_load.wait()

    def turn(p):
        def gather_own(c, carry):
            own_col = pl.multiple_of(owns[p] * blk, blk)
            at = pl.ds(pl.multiple_of(c * rows + p * piece, piece), piece)
            span = pl.ds(p * piece, piece)
            LR[0, at, :] = act_raw[c, span, pl.ds(own_col, blk)].astype(jnp.float32)
            LR[1, at, :] = second_of(
                p, lambda b: act_raw[c, span, b * blk : (b + 1) * blk].astype(jnp.float32)
            )
            return carry

        lax.fori_loop(0, pc, gather_own, 0, unroll=4)

        def spread(k, carry):
            for hf in range(halves):
                X[hf, k, mine] = LR[hf, pl.ds(k, pc, stride=rows), :].astype(jnp.bfloat16)
            return carry

        lax.fori_loop(p * piece, (p + 1) * piece, spread, 0, unroll=4)

    def act_slab(p, c):
        return X.at[:, pl.ds(p * piece, piece), c]

    y_copies, c_copies, f_copies = [], [], []
    for p in range(pieces):
        turn(p)
        slab = act_slab(p, mine)
        y = remote(slab, slab, ys.at[p], yr.at[p], me, flipped)
        y.start()
        c = remote(slab, slab, cs.at[p], cr.at[p], me, core)
        c.start()
        y_copies.append(y)
        c_copies.append(c)

    inv_chan = 1.0 / (pc * chans)

    def ahead(p):
        def body(i, carry):
            ks = [p * piece + 2 * i + u for u in range(2)]
            views = [(hf, k) for k in ks for hf in range(halves)]
            stands, normed, invs = [], [], []
            for hf, k in views:
                x = X[hf, k].reshape(pc * chans, blk).astype(jnp.float32)
                mean = jnp.sum(x, axis=0, keepdims=True) * inv_chan
                square = jnp.sum(x * x, axis=0, keepdims=True) * inv_chan
                inv = lax.rsqrt(square - mean * mean + EPS)
                standard = (x - mean) * inv
                invs.append(inv)
                stands.append(standard.astype(jnp.bfloat16))
                normed.append((standard * gain_ref[...] + bias_ref[...]).astype(jnp.bfloat16))
            projected = dot(wt_ref[...], jnp.concatenate(normed, axis=1))
            for u, (hf, k) in enumerate(views):
                INV[hf, pl.ds(k, 1), :] = invs[u]
                X[hf, k] = stands[u].reshape(chans, pc, blk)
                Nn[hf, k] = normed[u].reshape(chans, pc, blk)
                part = projected[:, u * blk : (u + 1) * blk]
                ls = jax.nn.sigmoid(part[:pc])
                ll = part[pc : 2 * pc]
                rsig = jax.nn.sigmoid(part[2 * pc : 3 * pc])
                rl = part[3 * pc :]
                Pm[hf, k, 0:pc] = ls
                Pm[hf, k, pc : 2 * pc] = ll
                Pm[hf, k, 2 * pc : 3 * pc] = rsig
                Pm[hf, k, 3 * pc :] = rl
                lv, rv = ls * ll, rsig * rl
                if hf == 1:
                    lv, rv = lv * paired[p], rv * paired[p]
                LR[hf, pl.ds(k, pc, stride=rows), :] = lv
                LR[hf, pl.ds(pc * rows + k, pc, stride=rows), :] = rv
            return carry

        lax.fori_loop(0, piece // 2, body, 0)

    def arrive(p):
        y_copies[p].wait_recv()
        slab = act_slab(p, flipped)
        f = remote(slab, slab, fs.at[p], fr.at[p], me, core)
        f.start()
        f_copies.append(f)
        c_copies[p].wait_recv()
        f.wait_recv()
        y_copies[p].wait_send()
        c_copies[p].wait_send()
        f.wait_send()

    arrive(0)
    ahead(0)
    forward(2, 0)
    arrive(1)
    ahead(1)
    forward(2, 1)
    for p in range(2, pieces):
        arrive(p)
        ahead(p)
    forward(3, 0)
    forward(3, 1)

    for way in (0, 1):
        @pl.when(by_chord(me, way, top - 1))
        def _(way=way):
            for ch in range(CHUNKS):
                ring_copy(way, top - 1, ch).wait_recv()
        for p in range(pieces):
            @pl.when(gets_window(way, p))
            def _(way=way, p=p):
                window_copy(way, p).wait_recv()
    if cross:
        cross_load.wait()

    def lr_rows(which, h, p):
        return pl.ds(pl.multiple_of((which * pc + h) * rows + p * piece, piece), piece)

    def near(p, h):
        own_at = pl.ds(pl.multiple_of(owns[p] * blk, blk), blk)
        win_at = pl.ds(pl.multiple_of(owns[p] * blk - row_first + rows, piece), blk)
        tl, tri = Dall[h, own_at, :], Ow[h, win_at, :]
        l0 = LR[0, lr_rows(0, h, p), :].astype(jnp.bfloat16)
        r0 = LR[0, lr_rows(1, h, p), :].astype(jnp.bfloat16)
        r1 = LR[1, lr_rows(1, h, p), :].astype(jnp.bfloat16)
        gl = dot_t(r0, tl) + dot_t(r1, tri)
        gr = dot(l0, jnp.concatenate([tl, tri], axis=1))
        gr0, over = gr[:, :blk], None
        if cross:
            l1 = LR[1, lr_rows(0, h, p), :].astype(jnp.bfloat16)
            gr0 = gr0 + dot(l1, BL[h, p])
            over = dot_t(r0, BL[h, p])
        return gl, gr0, gr[:, blk:], over

    def run_near(p):
        def body(i, carry):
            results = [(2 * i + u, near(p, 2 * i + u)) for u in range(2)]
            for h, (gl, gr0, gx, over) in results:
                at = pl.ds(pl.multiple_of(h * rows + p * piece, piece), piece)
                LR[0, lr_rows(0, h, p), :] = gl
                LR[0, lr_rows(1, h, p), :] = gr0
                GX[at, :] = gx
                if cross:
                    GY[at, :] = over
            return carry

        lax.fori_loop(0, pc // 2, body, 0)

    def distant(h, carry):
        results = []
        for p in range(pieces):
            br = second_of(p, lambda b: Dall[h, b * blk : (b + 1) * blk, :])
            l1 = LR[1, lr_rows(0, h, p), :].astype(jnp.bfloat16)
            r1 = LR[1, lr_rows(1, h, p), :].astype(jnp.bfloat16)
            at = pl.ds(pl.multiple_of(h * rows + p * piece, piece), piece)
            gl = dot_t(r1, br)
            if cross:
                gl = gl + GY[at, :]
            results.append((gl, GX[at, :] + dot(l1, br)))
        for p, (gl, gr) in enumerate(results):
            LR[1, lr_rows(0, h, p), :] = gl
            LR[1, lr_rows(1, h, p), :] = gr
        return carry

    def run_distant(ch):
        size = pc // CHUNKS
        lax.fori_loop(ch * size, (ch + 1) * size, distant, 0)

    WA[...] = jnp.zeros_like(WA)
    GA[...] = jnp.zeros_like(GA)

    def back(hf, p):
        def body(i, carry):
            grads, total = [], None
            ks = [p * piece + UNROLL * i + u for u in range(UNROLL)]
            for k in ks:
                gl = LR[hf, pl.ds(k, pc, stride=rows), :]
                gr = LR[hf, pl.ds(pc * rows + k, pc, stride=rows), :]
                if hf == 1:
                    gl, gr = gl * paired[p], gr * paired[p]
                ls, ll = Pm[hf, k, 0:pc], Pm[hf, k, pc : 2 * pc]
                rsig, rl = Pm[hf, k, 2 * pc : 3 * pc], Pm[hf, k, 3 * pc :]
                a, b = gl * ls, gr * rsig
                g = jnp.concatenate([a * ll * (1.0 - ls), a, b * rl * (1.0 - rsig), b], axis=0)
                total = g if total is None else total + g
                grads.append(g.astype(jnp.bfloat16))
            pair = jnp.concatenate(grads, axis=1)
            partial = dot(wb_ref[...], pair)
            stands = [X[hf, k].reshape(pc * chans, blk) for k in ks]
            both = jnp.concatenate(
                [
                    jnp.concatenate([Nn[hf, k].reshape(pc * chans, blk), st], axis=0)
                    for k, st in zip(ks, stands)
                ],
                axis=1,
            )
            weights = dot_t(pair, both)
            for u, (k, st) in enumerate(zip(ks, stands)):
                n = partial[:, u * blk : (u + 1) * blk]
                scaled = n * gain_ref[...]
                S[hf, 0, pl.ds(k, 1), :] = jnp.sum(scaled, axis=0, keepdims=True)
                S[hf, 1, pl.ds(k, 1), :] = jnp.sum(scaled * st.astype(jnp.float32), axis=0, keepdims=True)
                Nn[hf, k] = n.astype(jnp.bfloat16).reshape(chans, pc, blk)
            WA[...] += weights
            GA[...] += total
            return carry

        lax.fori_loop(0, piece // UNROLL, body, 0)

    def span_of(p):
        return pl.ds(p * piece, piece)

    def core_copies(hf, p):
        at = span_of(p)
        return [
            remote(Nn.at[hf, at, core], RC.at[0, hf, at], qs.at[hf, p, 0], qr.at[hf, p, 0], me, core),
            remote(Nn.at[hf, at, far], RC.at[1, hf, at], qs.at[hf, p, 1], qr.at[hf, p, 1], me, core),
            remote(S.at[hf, :, at], SR.at[hf, :, at], ts.at[hf, p], tr.at[hf, p], me, core),
        ]

    def y_back(hf, p):
        at = span_of(p)
        return [
            remote(YS.at[hf, at], YR.at[hf, at], us.at[hf, p], ur.at[hf, p], me, flipped),
            remote(SB.at[hf, :, at], SY.at[hf, :, at], zs.at[hf, p], zr.at[hf, p], me, flipped),
        ]

    def combine(hf, p):
        for c in core_copies(hf, p):
            c.wait_recv()
        at = span_of(p)
        YS[hf, at] = (
            Nn[hf, at, flipped].astype(jnp.float32) + RC[1, hf, at].astype(jnp.float32)
        ).astype(jnp.bfloat16)
        total = S[hf, :, at, :] + SR[hf, :, at, :]
        SR[hf, :, at, :] = total
        SB[hf, :, at, :] = total.astype(jnp.bfloat16)
        for c in y_back(hf, p):
            c.start()

    scale = 1.0 / (pc * chans)

    def finish(hf, p):
        for c in y_back(hf, p):
            c.wait_recv()
        at = span_of(p)
        SR[hf, :, at, :] = (SR[hf, :, at, :] + SY[hf, :, at, :].astype(jnp.float32)) * scale
        gain = gain_ref[pl.ds(pl.multiple_of(mine * pc, pc), pc), :]

        def body(k, carry):
            n = (
                Nn[hf, k, mine].astype(jnp.float32)
                + RC[0, hf, k].astype(jnp.float32)
                + YR[hf, k].astype(jnp.float32)
            )
            st = X[hf, k, mine].astype(jnp.float32)
            s0 = SR[hf, 0, pl.ds(k, 1), :]
            s1 = SR[hf, 1, pl.ds(k, 1), :]
            out = (n * gain - s0 - st * s1) * INV[hf, pl.ds(k, 1), :]
            LR[hf, pl.ds(k, pc, stride=rows), :] = out
            return carry

        lax.fori_loop(p * piece, (p + 1) * piece, body, 0, unroll=4)

        def put(c, carry):
            rows_at = pl.ds(pl.multiple_of(c * rows + p * piece, piece), piece)
            pg_ref[hf, c, at, :] = LR[hf, rows_at, :].astype(jnp.bfloat16)
            return carry

        lax.fori_loop(0, pc, put, 0, unroll=4)

    items = [(hf, p) for hf in range(halves) for p in range(pieces)]

    def launch(hf, p):
        back(hf, p)
        for c in core_copies(hf, p):
            c.start()

    for p in range(pieces):
        run_near(p)
        launch(0, p)
        if p > 0:
            combine(0, p - 1)
            for way in (0, 1):
                forward(4, way, range((p - 1) * CHUNKS // 2, p * CHUNKS // 2))
    combine(0, pieces - 1)
    for p in range(pieces - 1):
        finish(0, p)
    for ch in range(CHUNKS):
        for way in (0, 1):
            forward(top + 1, way, [ch])
        run_distant(ch)
    for p in range(pieces):
        launch(1, p)
        if p > 0:
            combine(1, p - 1)
    combine(1, pieces - 1)

    allc = pc * chans
    wide = wt_ref[...].astype(jnp.float32)
    gain_term = jnp.sum(wide * WA[:, allc:], axis=0, keepdims=True)
    bias_term = jnp.sum(wide * jnp.sum(GA[...], axis=1, keepdims=True), axis=0, keepdims=True)
    sub = lax.broadcasted_iota(jnp.int32, (8, allc), 0)
    WS[me, : 4 * pc, :] = WA[:, :allc]
    WS[me, 4 * pc :, :] = jnp.where(sub == 0, gain_term, jnp.where(sub == 1, bias_term, 0.0))

    def wide_copy(hop):
        return remote(
            WS.at[me], WS.at[me], wbs.at[hop - 1], wbr.at[hop - 1], (me + hop) % ring, mine
        )

    for hop in range(1, ring):
        wide_copy(hop).start()

    finish(0, pieces - 1)

    for hop in range(1, ring):
        wide_copy(hop).wait_recv()
    summed = WS[0]
    for d in range(1, ring):
        summed = summed + WS[d]
    summed = summed * (1.0 / width)
    wsum_ref[...] = summed[: 4 * pc]
    VS[mine] = summed[4 * pc :]

    def vec_copy(hop):
        return remote(VS.at[mine], VS.at[mine], vs.at[hop - 1], vr.at[hop - 1], me, (mine + hop) % chans)

    for hop in range(1, chans):
        vec_copy(hop).start()
    for p in range(pieces):
        finish(1, p)
    for hop in range(1, chans):
        vec_copy(hop).wait_recv()
    total = VS[0]
    for d in range(1, chans):
        total = total + VS[d]
    vec_ref[...] = total

    for way in (0, 1):
        for p in range(pieces):
            @pl.when(sends_window(way, p))
            def _(way=way, p=p):
                window_copy(way, p).wait_send()
    for step in range(1, top + 1):
        for ch in range(CHUNKS):
            for way in ways_of(step, ch):
                ring_sent(way, step, ch)
    for way in (0, 1):
        @pl.when(chord_sends(way))
        def _(way=way):
            for ch in range(CHUNKS):
                chord_copy(way, ch).wait_send()
    for hf, p in items:
        for c in core_copies(hf, p) + y_back(hf, p):
            c.wait_send()
    for hop in range(1, ring):
        wide_copy(hop).wait_send()
    for hop in range(1, chans):
        vec_copy(hop).wait_send()


def call_mega(cross, dims, contact, act, cot, gates, gain, bias, *extra):
    chans, ring, pc, rows, piece, pieces, blk, width = dims
    allc = pc * chans
    bf, f32 = jnp.bfloat16, jnp.float32
    V, D = pltpu.VMEM, pltpu.SemaphoreType.DMA
    top = ring // 2
    scratch = [
        V((pc, rows, width), bf), V((pc, rows, width), bf),
        V((2, rows, chans, pc, blk), bf), V((2, rows, chans, pc, blk), bf),
        V((2, rows, 4 * pc, blk), f32), V((2, 2 * pc * rows, blk), f32), V((pc * rows, blk), f32),
        V((pc, ring * rows, blk), bf), V((pc, 3 * rows, blk), bf),
        V((2, 2, rows, pc, blk), bf), V((2, rows, pc, blk), bf), V((2, rows, pc, blk), bf),
        V((2, rows, blk), f32), V((2, 2, rows, blk), f32), V((2, 2, rows, blk), f32),
        V((2, 2, rows, blk), bf), V((2, 2, rows, blk), bf),
        V((4 * pc, 2 * allc), f32), V((4 * pc, blk), f32),
        V((ring, 4 * pc + 8, allc), f32), V((chans, 8, allc), f32),
        V((4 * pc, allc), bf), V((allc, 4 * pc), bf), V((allc, blk), f32), V((allc, blk), f32),
        D((3,)), D((CHUNKS,)), D((pieces,)), D((pieces,)), D((pieces,)), D((pieces,)), D((pieces,)), D((pieces,)),
        D((2, top, CHUNKS)), D((2, top, CHUNKS)), D((2, pieces)), D((2, pieces)),
        D((2, pieces, 2)), D((2, pieces, 2)), D((2, pieces)), D((2, pieces)),
        D((2, pieces)), D((2, pieces)), D((2, pieces)), D((2, pieces)),
        D((ring - 1,)), D((ring - 1,)), D((chans - 1,)), D((chans - 1,)),
    ]
    if cross:
        scratch += [V((pc, pieces, blk, blk), bf), V((pc * rows, blk), f32)]
    vmem = pl.BlockSpec(memory_space=pltpu.VMEM)
    hbm = pl.BlockSpec(memory_space=pl.ANY)
    return pl.pallas_call(
        functools.partial(mega, cross, dims),
        out_shape=(
            jax.ShapeDtypeStruct((2, pc, rows, blk), bf),
            jax.ShapeDtypeStruct((4 * pc, allc), f32),
            jax.ShapeDtypeStruct((8, allc), f32),
        ),
        in_specs=[pl.BlockSpec(memory_space=pltpu.SMEM), hbm, hbm] + [vmem] * 6
        + [hbm] * len(extra),
        out_specs=(vmem, vmem, vmem),
        scratch_shapes=scratch,
        compiler_params=pltpu.CompilerParams(
            collective_id=2 if cross else 1, has_side_effects=True, vmem_limit_bytes=VMEM_BYTES
        ),
        name="triangle_cross" if cross else "triangle",
    )(contact, act, cot, *gates, gain, bias, *extra)


def expand(dims, contact_ref, pg_ref, wsum_ref, vec_ref, out_ref, g_ref, b_ref, *w_refs):
    chans, ring, pc, rows, piece, pieces, blk, width = dims
    row_first = lax.axis_index("rows") * rows
    for p in range(pieces):
        own = (row_first + p * piece) // blk
        at = pl.ds(p * piece, piece)
        near, far = pg_ref[0, :, at, :], pg_ref[1, :, at, :]
        none = jnp.zeros_like(near)
        for b in range(width // blk):
            held = jnp.where(contact_ref[own, b] > 0, far, none)
            out_ref[:, at, b * blk : (b + 1) * blk] = jnp.where(own == b, near, held)

    @pl.when(pl.program_id(0) == 0)
    def _():
        allc = pc * chans
        mine = lax.axis_index("chan")
        vec = pltpu.roll(vec_ref[...], (allc - mine * pc) % allc, 1)
        g_ref[...] = vec[0:1, :pc]
        b_ref[...] = vec[1:2, :pc]
        for i, ref in enumerate(w_refs):
            ref[...] = wsum_ref[i * pc : (i + 1) * pc, :]


def call_expand(dims, contact, pg, wsum, vec, steps=4):
    chans, ring, pc, rows, piece, pieces, blk, width = dims
    allc = pc * chans
    f32 = jnp.float32

    def whole(shape):
        return pl.BlockSpec(shape, lambda i: (0,) * len(shape))

    return pl.pallas_call(
        functools.partial(expand, dims),
        grid=(steps,),
        out_shape=(
            jax.ShapeDtypeStruct((pc, rows, width), pg.dtype),
            jax.ShapeDtypeStruct((1, pc), f32),
            jax.ShapeDtypeStruct((1, pc), f32),
        )
        + (jax.ShapeDtypeStruct((pc, allc), f32),) * 4,
        in_specs=[
            pl.BlockSpec(memory_space=pltpu.SMEM),
            pl.BlockSpec((2, pc // steps, rows, blk), lambda i: (0, i, 0, 0)),
            whole((4 * pc, allc)),
            whole((8, allc)),
        ],
        out_specs=(
            pl.BlockSpec((pc // steps, rows, width), lambda i: (i, 0, 0)),
            whole((1, pc)),
            whole((1, pc)),
        )
        + (whole((pc, allc)),) * 4,
        name="expand",
    )(contact, pg, wsum, vec)


def everywhere(x, rows, width, row_first):
    ring = lax.axis_size("rows")
    order = ring_order(ring)
    place = [order.index(d) for d in range(ring)]
    order_table = jnp.array(order, jnp.int32)
    my_place = jnp.array(place, jnp.int32)[lax.axis_index("rows")]
    right_perm = [(order[i], order[(i + 1) % ring]) for i in range(ring)]
    left_perm = [(order[(i + 1) % ring], order[i]) for i in range(ring)]
    half, top = x.shape[0] // 2, ring // 2
    out = jnp.zeros((x.shape[0], width, x.shape[2]), x.dtype)
    out = lax.dynamic_update_slice(out, x, (0, row_first, 0))
    going_right, going_left = x, x
    for step in range(1, top + 1):
        last = step == top and ring % 2 == 0
        if last:
            going_right, going_left = going_right[:half], going_left[half:]
        going_right = lax.ppermute(going_right, "rows", right_perm)
        going_left = lax.ppermute(going_left, "rows", left_perm)
        from_left = order_table[(my_place - step + ring) % ring] * rows
        from_right = order_table[(my_place + step) % ring] * rows
        out = lax.dynamic_update_slice(out, going_right, (0, from_left, 0))
        out = lax.dynamic_update_slice(out, going_left, (half if last else 0, from_right, 0))
    return out


def fused(
    pair_act, pair_cot, contact, ln_gain, ln_bias, left_gate, left_value, right_gate, right_value
):
    pc, rows, width = pair_act.shape
    blocks = contact.shape[0]
    blk = width // blocks
    chans, ring = lax.axis_size("chan"), lax.axis_size("rows")
    piece = math.gcd(rows, blk)
    pieces = rows // piece
    dims = (chans, ring, pc, rows, piece, pieces, blk, width)
    row_first = lax.axis_index("rows") * rows
    mutual = jnp.sum(contact * contact.T) > blocks
    gates = (left_gate.T, left_value.T, right_gate.T, right_value.T)
    args = (contact, pair_act, pair_cot, gates, ln_gain[None], ln_bias[None])

    def simple(args):
        return call_mega(False, dims, *args)

    def crossed(args):
        cot = args[2]
        numbers = jnp.arange(blocks, dtype=jnp.int32)
        paired = jnp.sum(contact, axis=1) > 1
        other = jnp.where(paired, jnp.sum(contact * numbers[None, :], axis=1) - numbers, numbers)
        owns = [(row_first + p * piece) // blk for p in range(pieces)]
        seconds = [other[own] for own in owns]
        part = jnp.concatenate(
            [
                lax.dynamic_slice(cot, (0, p * piece, seconds[p] * blk), (pc, piece, blk))
                for p in range(pieces)
            ],
            axis=1,
        )
        every = everywhere(part, rows, width, row_first)
        corners = []
        for p in range(pieces):
            own, second = owns[p], seconds[p]
            good = (second != own) & (other[second] == own)
            here = lax.dynamic_slice(every, (0, second * blk, 0), (pc, blk, blk))
            corners.append(jnp.where(good, here, jnp.zeros((), here.dtype)))
        return call_mega(True, dims, *args, jnp.stack(corners, axis=1))

    held = lax.cond(mutual, crossed, simple, args)
    out = call_expand(dims, contact, *held)
    return (out[0], out[1][0], out[2][0]) + tuple(w.T for w in out[3:])


def local(*arrays):
    pc, rows, width = arrays[0].shape
    blk = width // arrays[2].shape[0]
    piece = math.gcd(rows, blk)
    chans, ring = lax.axis_size("chan"), lax.axis_size("rows")
    fits = (
        piece % 16 == 0 and rows // piece == 3 and blk == pc * chans == 4 * pc and ring == 8
    )
    return fused(*arrays) if fits else plain(*arrays)


def solution(mesh):
    in_specs = (
        P("chan", "rows", None),
        P("chan", "rows", None),
        P(),
        P(),
        P(),
        P(None, "chan"),
        P(None, "chan"),
        P(None, "chan"),
        P(None, "chan"),
    )
    out_specs = (
        P("chan", "rows", None),
        P("chan"),
        P("chan"),
        P(None, "chan"),
        P(None, "chan"),
        P(None, "chan"),
        P(None, "chan"),
    )
    return jax.shard_map(local, mesh=mesh, in_specs=in_specs, out_specs=out_specs, check_vma=False)
```

```python
import functools
import math

import jax
import jax.numpy as jnp
from jax import lax
from jax.experimental import pallas as pl
from jax.experimental.pallas import tpu as pltpu
from jax.sharding import PartitionSpec as P

EPS = 1e-05


def ring_order(count):
    return list(range(0, count, 2)) + list(range(1, count, 2))[::-1]


def flip(x, axis, bit):
    count = lax.axis_size(axis)
    return lax.ppermute(x, axis, [(d, d ^ bit) for d in range(count)])


def bits_down(count):
    bits = [1 << b for b in range(count.bit_length() - 1)]
    return bits[::-1]


def plain(
    pair_act, pair_cot, contact, ln_gain, ln_bias, left_gate, left_value, right_gate, right_value
):
    part_chan, rows_here, width = pair_act.shape
    part_hid = pair_cot.shape[0]
    blocks = contact.shape[0]
    block_len = width // blocks
    chans = lax.axis_size("chan")
    ring = lax.axis_size("rows")
    all_chan = part_chan * chans
    mine = lax.axis_index("chan")
    row_first = lax.axis_index("rows") * rows_here
    piece = math.gcd(rows_here, block_len)
    pieces = rows_here // piece

    numbers = jnp.arange(blocks, dtype=jnp.int32)
    other = jnp.sum(contact * numbers[None, :], axis=1) - numbers
    paired = jnp.sum(contact, axis=1) > 1
    row_block = (row_first + jnp.arange(rows_here, dtype=jnp.int32)) // block_len
    at_own = row_block[:, None] == numbers[None, :]
    row_other = jnp.sum(jnp.where(at_own, other[None, :], 0), axis=1)
    row_paired = jnp.sum(jnp.where(at_own, paired[None, :].astype(jnp.int32), 0), axis=1) > 0
    at_other = (row_other[:, None] == numbers[None, :]) & row_paired[:, None]
    weight = jnp.concatenate(
        [
            jnp.ones((rows_here, block_len), jnp.float32),
            jnp.broadcast_to(
                row_paired.astype(jnp.float32)[:, None], (rows_here, block_len)
            ),
        ],
        axis=1,
    )

    def compact(x):
        def pick(at):
            out = jnp.zeros((x.shape[0], rows_here, block_len), x.dtype)
            for b in range(blocks):
                here = x[:, :, b * block_len : (b + 1) * block_len]
                out = jnp.where(at[:, b][None, :, None], here, out)
            return out

        return jnp.concatenate([pick(at_own), pick(at_other)], axis=2)

    cot = compact(pair_cot)
    own_cot, other_cot = cot[:, :, :block_len], cot[:, :, block_len:]
    order = ring_order(ring)
    place = [order.index(d) for d in range(ring)]
    order_table = jnp.array(order, jnp.int32)
    my_place = jnp.array(place, jnp.int32)[lax.axis_index("rows")]
    right_perm = [(order[i], order[(i + 1) % ring]) for i in range(ring)]
    left_perm = [(order[(i + 1) % ring], order[i]) for i in range(ring)]
    act = compact(pair_act)

    def go_round(x):
        half = x.shape[0] // 2
        top = ring // 2
        arrived = []
        going_right, going_left = x, x
        for step in range(1, top + 1):
            last = step == top and ring % 2 == 0
            if last:
                going_right, going_left = going_right[:half], going_left[half:]
            going_right = lax.ppermute(going_right, "rows", right_perm)
            going_left = lax.ppermute(going_left, "rows", left_perm)
            from_left = order_table[(my_place - step + ring) % ring] * rows_here
            from_right = order_table[(my_place + step) % ring] * rows_here
            arrived.append((going_right, 0, from_left))
            arrived.append((going_left, half if last else 0, from_right))
        here, _ = lax.optimization_barrier((x, arrived[0][0]))
        out = jnp.zeros((x.shape[0], width, x.shape[2]), x.dtype)
        out = lax.dynamic_update_slice(out, here, (0, row_first, 0))
        for block, first, at in arrived:
            out = lax.dynamic_update_slice(out, block, (first, at, 0))
        return out

    gathered = go_round(own_cot)
    reach = -(-(block_len - piece) // rows_here)
    window = [other_cot]
    for hop in range(1, min(reach, ring - 1) + 1):
        up = [(d, d + hop) for d in range(ring - hop)]
        down = [(d + hop, d) for d in range(ring - hop)]
        window = (
            [lax.ppermute(other_cot, "rows", up)]
            + window
            + [lax.ppermute(other_cot, "rows", down)]
        )
    window_first = row_first - (len(window) // 2) * rows_here
    window = jnp.concatenate(window, axis=1)
    owns = [(row_first + p * piece) // block_len for p in range(pieces)]
    seconds = [other[own] for own in owns]
    mutual_row = paired & paired[other] & (other[other] == numbers)

    def crossed(x):
        everywhere = go_round(x)
        return [
            jnp.where(
                mutual_row[own],
                lax.dynamic_slice(
                    everywhere, (0, second * block_len, 0), (part_hid, block_len, block_len)
                ),
                jnp.zeros((), x.dtype),
            )
            for own, second in zip(owns, seconds)
        ]

    def uncrossed(x):
        return [jnp.zeros((part_hid, block_len, block_len), x.dtype) for _ in owns]

    cross = lax.cond(jnp.any(mutual_row), crossed, uncrossed, other_cot)

    parts, offsets = [act], [0]
    for bit in bits_down(chans):
        parts = parts + [flip(x, "chan", bit) for x in parts]
        offsets = offsets + [o + bit for o in offsets]
    full_act = jnp.concatenate(parts, axis=0).astype(jnp.float32)
    partner = jnp.array(offsets, jnp.int32) ^ mine

    def by_partner(x):
        return x.reshape((chans, part_chan) + x.shape[1:])[partner].reshape(x.shape)

    slot_of = [offsets.index(o) for o in range(chans)]
    back_order = jnp.array(slot_of, jnp.int32)[jnp.arange(chans, dtype=jnp.int32) ^ mine]

    def by_channel(x):
        return x.reshape((chans, part_chan) + x.shape[1:])[back_order].reshape(x.shape)

    gain = by_partner(ln_gain)
    bias = by_partner(ln_bias)
    w_stacked = by_partner(
        jnp.concatenate([left_gate, left_value, right_gate, right_value], axis=1)
    )

    mean = jnp.mean(full_act, axis=0)
    inv_std = lax.rsqrt(jnp.mean(full_act * full_act, axis=0) - mean * mean + EPS)
    standard = (full_act - mean) * inv_std
    normed = (standard * gain[:, None, None] + bias[:, None, None]).astype(jnp.bfloat16)
    standard_near = standard.astype(jnp.bfloat16)
    projected = jnp.einsum("ch,ckn->hkn", w_stacked, normed, preferred_element_type=jnp.float32)
    left_logit, left_linear, right_logit, right_linear = jnp.split(projected, 4, axis=0)
    left_sigmoid = jax.nn.sigmoid(left_logit)
    right_sigmoid = jax.nn.sigmoid(right_logit)
    left = (weight * left_sigmoid * left_linear).astype(jnp.bfloat16)
    right = (weight * right_sigmoid * right_linear).astype(jnp.bfloat16)

    corners = []
    for own, second, back_cross in zip(owns, seconds, cross):
        size = (part_hid, block_len, block_len)
        top = jnp.concatenate(
            [
                lax.dynamic_slice(gathered, (0, own * block_len, 0), size),
                lax.dynamic_slice(window, (0, own * block_len - window_first, 0), size),
            ],
            axis=2,
        )
        low = jnp.concatenate(
            [back_cross, lax.dynamic_slice(gathered, (0, second * block_len, 0), size)], axis=2
        )
        corners.append(jnp.concatenate([top, low], axis=1))
    corner = jnp.stack(corners, axis=1)

    def cut(x):
        return x.reshape(part_hid, pieces, piece, 2 * block_len)

    grad_left = jnp.einsum(
        "hpkj,hpij->hpki", cut(right), corner, preferred_element_type=jnp.float32
    ).reshape(left.shape)
    grad_right = jnp.einsum(
        "hpki,hpij->hpkj", cut(left), corner, preferred_element_type=jnp.float32
    ).reshape(left.shape)
    keep_left = grad_left * weight
    keep_right = grad_right * weight
    grads = jnp.concatenate(
        [
            (keep_left * left_linear * left_sigmoid * (1.0 - left_sigmoid)).astype(jnp.bfloat16),
            (keep_left * left_sigmoid).astype(jnp.bfloat16),
            (keep_right * right_linear * right_sigmoid * (1.0 - right_sigmoid)).astype(
                jnp.bfloat16
            ),
            (keep_right * right_sigmoid).astype(jnp.bfloat16),
        ],
        axis=0,
    )

    def back(rows):
        return jnp.einsum("ch,hkn->ckn", rows, grads, preferred_element_type=jnp.float32)

    w_parts = {o: w_stacked[i * part_chan : (i + 1) * part_chan] for i, o in enumerate(offsets)}
    partial = {o: back(w_parts[o]) for o in offsets}
    first_sum = jnp.zeros(mean.shape, jnp.float32)
    second_sum = jnp.zeros(mean.shape, jnp.float32)
    for i, o in enumerate(offsets):
        span = slice(i * part_chan, (i + 1) * part_chan)
        scaled = partial[o] * gain[span][:, None, None]
        first_sum = first_sum + jnp.sum(scaled, axis=0)
        second_sum = second_sum + jnp.sum(scaled * standard[span], axis=0)
    sums = jnp.stack([first_sum, second_sum])
    late_grads = grads
    for bit in bits_down(chans)[::-1]:
        leaving = {o: partial[o].astype(jnp.bfloat16) for o in partial if o & bit}
        received = {o - bit: flip(x, "chan", bit) for o, x in leaving.items()}
        late_grads, _ = lax.optimization_barrier((late_grads, tuple(leaving.values())))
        partial = {o: partial[o] + x.astype(jnp.float32) for o, x in received.items()}
        sums = sums + flip(sums, "chan", bit)
    normed_grad = partial[0]
    scaled = normed_grad * gain[:part_chan][:, None, None]
    pair_grad = (
        (scaled - sums[0] / all_chan - standard[:part_chan] * (sums[1] / all_chan)) * inv_std
    ).astype(jnp.bfloat16)
    near, far = pair_grad[:, :, :block_len], pair_grad[:, :, block_len:]
    none = jnp.zeros((), pair_grad.dtype)
    pair_grad = jnp.concatenate(
        [
            jnp.where(
                at_own[:, b][None, :, None],
                near,
                jnp.where(at_other[:, b][None, :, None], far, none),
            )
            for b in range(blocks)
        ],
        axis=2,
    )

    weight_total = jnp.einsum("ckn,hkn->ch", normed, late_grads, preferred_element_type=jnp.float32)
    moment = jnp.einsum("ckn,hkn->ch", standard_near, late_grads, preferred_element_type=jnp.float32)
    wide = w_stacked.astype(jnp.float32)
    gain_terms = jnp.sum(wide * moment, axis=1)
    bias_terms = jnp.sum(wide * jnp.sum(late_grads.astype(jnp.float32), axis=(1, 2))[None, :], axis=1)
    vectors = by_channel(jnp.stack([gain_terms, bias_terms], axis=1))
    for bit in bits_down(chans):
        vectors = vectors + flip(vectors, "chan", bit)
    vectors = lax.dynamic_slice_in_dim(vectors, mine * part_chan, part_chan, 0)
    for bit in bits_down(ring):
        vectors = vectors + flip(vectors, "rows", bit)
        weight_total = weight_total + flip(weight_total, "rows", bit)
    factor = 1.0 / width
    weight_total = by_channel(weight_total) * factor
    vectors = vectors * factor
    return (pair_grad, vectors[:, 0], vectors[:, 1]) + tuple(jnp.split(weight_total, 4, axis=1))


MESH = pl.DeviceIdType.MESH
VMEM_BYTES = 66 << 20
CHUNKS = 4
LAST_LEFT = 1
UNROLL = 4


def dot(a, b):
    return lax.dot_general(a, b, (((1,), (0,)), ((), ())), preferred_element_type=jnp.float32)


def dot_t(a, b):
    return lax.dot_general(a, b, (((1,), (1,)), ((), ())), preferred_element_type=jnp.float32)


def ring_at(place, ring):
    late = place // (ring // 2)
    return (1 - late) * 2 * place + late * (2 * (ring - 1 - place) + 1)


def ring_place(d, ring):
    return (1 - d % 2) * (d // 2) + (d % 2) * (ring - 1 - d // 2)


def mega(cross, dims, contact_ref, act_hbm, cot_hbm, lg_ref, lv_ref, rg_ref, rv_ref, g_ref, b_ref, *rest):
    chans, ring, pc, rows, piece, pieces, blk, width = dims
    (
        pg_ref, wsum_ref, vec_ref,
        act_raw, cot_raw, X, Nn, Pm, LR, GX, Dall, Ow, RC, YS, YR, INV, S, SR, SB, SY,
        WA, GA, WS, VS, wt_ref, wb_ref, gain_ref, bias_ref,
        ld, ch_s, ys, yr, cs, cr, fs, fr, rs, rr, os_, or_, qs, qr, ts, tr, us, ur, zs, zr, wbs, wbr, vs, vr,
    ) = rest[:52]
    me = lax.axis_index("rows")
    mine = lax.axis_index("chan")
    core = mine + 1 - 2 * (mine % 2)
    flipped = (mine + chans // 2) % chans
    far = core + 0
    far = (core + chans // 2) % chans
    row_first = me * rows
    place = ring_place(me, ring)
    right = ring_at((place + 1) % ring, ring)
    left = ring_at((place + ring - 1) % ring, ring)
    halves = 2
    owns = [(row_first + p * piece) // blk for p in range(pieces)]

    blocks = width // blk
    picks, paired, mutual = [], [], []
    for p in range(pieces):
        active = [contact_ref[owns[p], b] for b in range(blocks)]
        picks.append([(active[b] > 0) & (owns[p] != b) for b in range(blocks)])
        both = [
            active[b] * contact_ref[b, owns[p]] * (owns[p] != b).astype(jnp.int32)
            for b in range(blocks)
        ]
        mutual.append(sum(both[1:], both[0]).astype(jnp.float32))
        paired.append((sum(active[1:], active[0]) - 1).astype(jnp.float32))

    def second_of(p, read):
        out = read(0)
        for b in range(1, blocks):
            out = jnp.where(picks[p][b], read(b), out)
        return out

    loads = []
    cot_load = pltpu.make_async_copy(cot_hbm, cot_raw, ld.at[0])
    cot_load.start()
    act_load = pltpu.make_async_copy(act_hbm, act_raw, ld.at[1])
    act_load.start()

    barrier = pltpu.get_barrier_semaphore()
    for hop in range(1, ring):
        pl.semaphore_signal(barrier, inc=1, device_id=((me + hop) % ring, mine), device_id_type=MESH)
    for hop in range(1, chans):
        pl.semaphore_signal(barrier, inc=1, device_id=(me, (mine + hop) % chans), device_id_type=MESH)
    pl.semaphore_wait(barrier, ring - 1 + chans - 1)

    def remote(src, dst, send, recv, r, c):
        return pltpu.make_async_remote_copy(
            src_ref=src, dst_ref=dst, send_sem=send, recv_sem=recv,
            device_id=(r, c), device_id_type=MESH,
        )

    cot_load.wait()

    def pick_cot(h, carry):
        for p in range(pieces):
            span = pl.ds(p * piece, piece)
            own_col = pl.multiple_of(owns[p] * blk, blk)
            at = pl.ds(pl.multiple_of(row_first + p * piece, piece), piece)
            Dall[h, at, :] = cot_raw[h, span, pl.ds(own_col, blk)]
            other = paired[p] * second_of(
                p, lambda b: cot_raw[h, span, b * blk : (b + 1) * blk].astype(jnp.float32)
            )
            there = at if cross else pl.ds(rows + p * piece, piece)
            Ow[h, there, :] = other.astype(jnp.bfloat16)
        return carry

    rings = [Dall, Ow] if cross else [Dall]

    def ring_copy(way, step, ch, kind=0):
        if way == 0:
            unit, to = ring_at((place - (step - 1) + ring) % ring, ring), right
        else:
            unit, to = ring_at((place + (step - 1)) % ring, ring), left
        size = pc // CHUNKS
        span = pl.ds(pl.multiple_of(unit * rows, rows), rows)
        view = rings[kind].at[pl.ds(ch * size, size), span]
        return remote(
            view, view, rs.at[kind, way, step - 1, ch], rr.at[kind, way, step - 1, ch], to, mine
        )

    top = ring // 2

    def ways_of(step, ch):
        if step < top:
            return [0, 1]
        return [1] if ch >= CHUNKS - LAST_LEFT else [0]

    def pair_of(d):
        return d + 1 - 2 * (d % 2)

    def has_chord(d):
        return (d // 2 > 0) & (d // 2 < ring // 2 - 1)

    def chord_way(d):
        return (d % 2 + d // (ring // 2)) % 2

    def by_chord(d, way, step):
        if step != top - 1:
            return None
        return has_chord(d) & (chord_way(d) == way)

    def chord_copy(way, ch, kind):
        size = pc // CHUNKS
        span = pl.ds(pl.multiple_of(me * rows, rows), rows)
        view = rings[kind].at[pl.ds(ch * size, size), span]
        return remote(
            view, view, ch_s.at[kind, ch], rr.at[kind, way, top - 2, ch], pair_of(me), mine
        )

    def chord_sends(way):
        return has_chord(me) & (chord_way(pair_of(me)) == way)

    def unless(condition, act):
        if condition is None:
            act()
        else:
            pl.when(jnp.logical_not(condition))(act)

    def ring_start(way, step, ch, kind):
        unless(
            by_chord(right if way == 0 else left, way, step),
            lambda: ring_copy(way, step, ch, kind).start(),
        )

    def ring_sent(way, step, ch, kind):
        unless(
            by_chord(right if way == 0 else left, way, step),
            lambda: ring_copy(way, step, ch, kind).wait_send(),
        )

    def window_copy(way, p):
        to = (me + 1) % ring if way == 0 else (me + ring - 1) % ring
        src = Ow.at[:, pl.ds(rows + p * piece, piece)]
        dst = Ow.at[:, pl.ds((0 if way == 0 else 2 * rows) + p * piece, piece)]
        return remote(src, dst, os_.at[way, p], or_.at[way, p], to, mine)

    def first_own(d):
        return (d * rows) // blk

    def last_own(d):
        return (d * rows + rows - piece) // blk

    def sends_window(way, p):
        if way == 0:
            return (me < ring - 1) & (owns[p] == first_own(me + 1))
        return (me > 0) & (owns[p] == last_own(me - 1))

    def gets_window(way, p):
        if way == 0:
            return (me > 0) & (((me - 1) * rows + p * piece) // blk == first_own(me))
        return (me < ring - 1) & (((me + 1) * rows + p * piece) // blk == last_own(me))

    def run_pick():
        lax.fori_loop(0, pc, pick_cot, 0, unroll=2)

    run_pick()
    for kind in range(len(rings)):
        for ch in range(CHUNKS):
            for way in (0, 1):
                ring_copy(way, 1, ch, kind).start()
        for way in (0, 1):
            @pl.when(chord_sends(way))
            def _(way=way, kind=kind):
                for ch in range(CHUNKS):
                    chord_copy(way, ch, kind).start()

    def windows(condition, act):
        for way in (0, 1):
            for p in range(0 if cross else pieces):
                @pl.when(condition(way, p))
                def _(way=way, p=p):
                    act(window_copy(way, p))

    windows(sends_window, lambda c: c.start())

    def forward(step, way, chunks=range(CHUNKS), kind=0):
        for ch in chunks:
            if way in ways_of(step - 1, ch):
                unless(
                    by_chord(me, way, step - 1),
                    lambda: ring_copy(way, step - 1, ch, kind).wait_recv(),
                )
            if step <= top and way in ways_of(step, ch):
                ring_start(way, step, ch, kind)

    for i, ref in enumerate((lg_ref, lv_ref, rg_ref, rv_ref)):
        wt_ref[i * pc : (i + 1) * pc, :] = ref[...]
    wb_ref[...] = jnp.transpose(wt_ref[...].astype(jnp.float32)).astype(jnp.bfloat16)
    square = (pc * chans, blk)
    gain_ref[...] = jnp.transpose(jnp.broadcast_to(g_ref[...], square))
    bias_ref[...] = jnp.transpose(jnp.broadcast_to(b_ref[...], square))

    act_load.wait()

    def turn(p):
        def gather_own(c, carry):
            own_col = pl.multiple_of(owns[p] * blk, blk)
            at = pl.ds(pl.multiple_of(c * rows + p * piece, piece), piece)
            span = pl.ds(p * piece, piece)
            LR[0, at, :] = act_raw[c, span, pl.ds(own_col, blk)].astype(jnp.float32)
            LR[1, at, :] = second_of(
                p, lambda b: act_raw[c, span, b * blk : (b + 1) * blk].astype(jnp.float32)
            )
            return carry

        lax.fori_loop(0, pc, gather_own, 0, unroll=4)

        def spread(k, carry):
            for hf in range(halves):
                X[hf, k, mine] = LR[hf, pl.ds(k, pc, stride=rows), :].astype(jnp.bfloat16)
            return carry

        lax.fori_loop(p * piece, (p + 1) * piece, spread, 0, unroll=4)

    def act_slab(p, c):
        return X.at[:, pl.ds(p * piece, piece), c]

    y_copies, c_copies, f_copies = [], [], []
    for p in range(pieces):
        turn(p)
        slab = act_slab(p, mine)
        y = remote(slab, slab, ys.at[p], yr.at[p], me, flipped)
        y.start()
        c = remote(slab, slab, cs.at[p], cr.at[p], me, core)
        c.start()
        y_copies.append(y)
        c_copies.append(c)

    inv_chan = 1.0 / (pc * chans)

    def ahead(p):
        def body(i, carry):
            ks = [p * piece + 2 * i + u for u in range(2)]
            views = [(hf, k) for k in ks for hf in range(halves)]
            stands, normed, invs = [], [], []
            for hf, k in views:
                x = X[hf, k].reshape(pc * chans, blk).astype(jnp.float32)
                mean = jnp.sum(x, axis=0, keepdims=True) * inv_chan
                square = jnp.sum(x * x, axis=0, keepdims=True) * inv_chan
                inv = lax.rsqrt(square - mean * mean + EPS)
                standard = (x - mean) * inv
                invs.append(inv)
                stands.append(standard.astype(jnp.bfloat16))
                normed.append((standard * gain_ref[...] + bias_ref[...]).astype(jnp.bfloat16))
            projected = dot(wt_ref[...], jnp.concatenate(normed, axis=1))
            for u, (hf, k) in enumerate(views):
                INV[hf, pl.ds(k, 1), :] = invs[u]
                X[hf, k] = stands[u].reshape(chans, pc, blk)
                Nn[hf, k] = normed[u].reshape(chans, pc, blk)
                part = projected[:, u * blk : (u + 1) * blk]
                ls = jax.nn.sigmoid(part[:pc])
                ll = part[pc : 2 * pc]
                rsig = jax.nn.sigmoid(part[2 * pc : 3 * pc])
                rl = part[3 * pc :]
                Pm[hf, k, 0:pc] = ls
                Pm[hf, k, pc : 2 * pc] = ll
                Pm[hf, k, 2 * pc : 3 * pc] = rsig
                Pm[hf, k, 3 * pc :] = rl
                lv, rv = ls * ll, rsig * rl
                if hf == 1:
                    lv, rv = lv * paired[p], rv * paired[p]
                LR[hf, pl.ds(k, pc, stride=rows), :] = lv
                LR[hf, pl.ds(pc * rows + k, pc, stride=rows), :] = rv
            return carry

        lax.fori_loop(0, piece // 2, body, 0)

    def arrive(p):
        y_copies[p].wait_recv()
        slab = act_slab(p, flipped)
        f = remote(slab, slab, fs.at[p], fr.at[p], me, core)
        f.start()
        f_copies.append(f)
        c_copies[p].wait_recv()
        f.wait_recv()
        y_copies[p].wait_send()
        c_copies[p].wait_send()
        f.wait_send()

    arrive(0)
    ahead(0)
    forward(2, 0)
    forward(2, 1)
    arrive(1)
    ahead(1)
    for p in range(2, pieces):
        arrive(p)
    forward(3, 0)
    for p in range(2, pieces):
        ahead(p)
    forward(3, 1)

    for way in (0, 1):
        @pl.when(by_chord(me, way, top - 1))
        def _(way=way):
            for kind in range(len(rings)):
                for ch in range(CHUNKS):
                    ring_copy(way, top - 1, ch, kind).wait_recv()
    windows(gets_window, lambda c: c.wait_recv())
    if cross:
        for step in range(2, top + 2):
            for way in (0, 1):
                forward(step, way, kind=1)
                if step > 3:
                    forward(step, way)

    def lr_rows(which, h, p):
        return pl.ds(pl.multiple_of((which * pc + h) * rows + p * piece, piece), piece)

    def near(p, h):
        own_at = pl.ds(pl.multiple_of(owns[p] * blk, blk), blk)
        win_first = 0 if cross else row_first - rows
        win_at = pl.ds(pl.multiple_of(owns[p] * blk - win_first, piece), blk)
        tl, tri = Dall[h, own_at, :], Ow[h, win_at, :]
        l0 = LR[0, lr_rows(0, h, p), :].astype(jnp.bfloat16)
        r0 = LR[0, lr_rows(1, h, p), :].astype(jnp.bfloat16)
        r1 = LR[1, lr_rows(1, h, p), :].astype(jnp.bfloat16)
        gl = dot_t(r0, tl) + dot_t(r1, tri)
        gr = dot(l0, jnp.concatenate([tl, tri], axis=1))
        gr0, over = gr[:, :blk], None
        if cross:
            l1 = LR[1, lr_rows(0, h, p), :].astype(jnp.bfloat16)
            low = second_of(p, lambda b: Ow[h, b * blk : (b + 1) * blk, :])
            gr0 = gr0 + mutual[p] * dot(l1, low)
            over = mutual[p] * dot_t(r0, low)
        return gl, gr0, gr[:, blk:], over

    def run_near(p):
        def body(i, carry):
            results = [(2 * i + u, near(p, 2 * i + u)) for u in range(2)]
            for h, (gl, gr0, gx, over) in results:
                at = pl.ds(pl.multiple_of(h * rows + p * piece, piece), piece)
                LR[0, lr_rows(0, h, p), :] = gl
                LR[0, lr_rows(1, h, p), :] = gr0
                GX[at, :] = gx
                if cross:
                    high = over.astype(jnp.bfloat16)
                    cot_raw[h, pl.ds(p * piece, piece), :blk] = high
                    cot_raw[h, pl.ds(p * piece, piece), blk : 2 * blk] = (
                        over - high.astype(jnp.float32)
                    ).astype(jnp.bfloat16)
            return carry

        lax.fori_loop(0, pc // 2, body, 0)

    def distant(h, carry):
        results = []
        for p in range(pieces):
            br = second_of(p, lambda b: Dall[h, b * blk : (b + 1) * blk, :])
            l1 = LR[1, lr_rows(0, h, p), :].astype(jnp.bfloat16)
            r1 = LR[1, lr_rows(1, h, p), :].astype(jnp.bfloat16)
            at = pl.ds(pl.multiple_of(h * rows + p * piece, piece), piece)
            gl = dot_t(r1, br)
            if cross:
                both = cot_raw[h, pl.ds(p * piece, piece), : 2 * blk].astype(jnp.float32)
                gl = gl + both[:, :blk] + both[:, blk:]
            results.append((gl, GX[at, :] + dot(l1, br)))
        for p, (gl, gr) in enumerate(results):
            LR[1, lr_rows(0, h, p), :] = gl
            LR[1, lr_rows(1, h, p), :] = gr
        return carry

    def run_distant(ch):
        size = pc // CHUNKS
        lax.fori_loop(ch * size, (ch + 1) * size, distant, 0)

    WA[...] = jnp.zeros_like(WA)
    GA[...] = jnp.zeros_like(GA)

    def back(hf, p):
        def body(i, carry):
            grads, total = [], None
            ks = [p * piece + UNROLL * i + u for u in range(UNROLL)]
            for k in ks:
                gl = LR[hf, pl.ds(k, pc, stride=rows), :]
                gr = LR[hf, pl.ds(pc * rows + k, pc, stride=rows), :]
                if hf == 1:
                    gl, gr = gl * paired[p], gr * paired[p]
                ls, ll = Pm[hf, k, 0:pc], Pm[hf, k, pc : 2 * pc]
                rsig, rl = Pm[hf, k, 2 * pc : 3 * pc], Pm[hf, k, 3 * pc :]
                a, b = gl * ls, gr * rsig
                g = jnp.concatenate([a * ll * (1.0 - ls), a, b * rl * (1.0 - rsig), b], axis=0)
                total = g if total is None else total + g
                grads.append(g.astype(jnp.bfloat16))
            pair = jnp.concatenate(grads, axis=1)
            partial = dot(wb_ref[...], pair)
            stands = [X[hf, k].reshape(pc * chans, blk) for k in ks]
            both = jnp.concatenate(
                [
                    jnp.concatenate([Nn[hf, k].reshape(pc * chans, blk), st], axis=0)
                    for k, st in zip(ks, stands)
                ],
                axis=1,
            )
            weights = dot_t(pair, both)
            for u, (k, st) in enumerate(zip(ks, stands)):
                n = partial[:, u * blk : (u + 1) * blk]
                scaled = n * gain_ref[...]
                S[hf, 0, pl.ds(k, 1), :] = jnp.sum(scaled, axis=0, keepdims=True)
                S[hf, 1, pl.ds(k, 1), :] = jnp.sum(scaled * st.astype(jnp.float32), axis=0, keepdims=True)
                Nn[hf, k] = n.astype(jnp.bfloat16).reshape(chans, pc, blk)
            WA[...] += weights
            GA[...] += total
            return carry

        lax.fori_loop(0, piece // UNROLL, body, 0)

    def span_of(p):
        return pl.ds(p * piece, piece)

    def core_copies(hf, p):
        at = span_of(p)
        return [
            remote(Nn.at[hf, at, core], RC.at[0, hf, at], qs.at[hf, p, 0], qr.at[hf, p, 0], me, core),
            remote(Nn.at[hf, at, far], RC.at[1, hf, at], qs.at[hf, p, 1], qr.at[hf, p, 1], me, core),
            remote(S.at[hf, :, at], SR.at[hf, :, at], ts.at[hf, p], tr.at[hf, p], me, core),
        ]

    def y_back(hf, p):
        at = span_of(p)
        return [
            remote(YS.at[hf, at], YR.at[hf, at], us.at[hf, p], ur.at[hf, p], me, flipped),
            remote(SB.at[hf, :, at], SY.at[hf, :, at], zs.at[hf, p], zr.at[hf, p], me, flipped),
        ]

    def combine(hf, p):
        for c in core_copies(hf, p):
            c.wait_recv()
        at = span_of(p)
        YS[hf, at] = (
            Nn[hf, at, flipped].astype(jnp.float32) + RC[1, hf, at].astype(jnp.float32)
        ).astype(jnp.bfloat16)
        total = S[hf, :, at, :] + SR[hf, :, at, :]
        SR[hf, :, at, :] = total
        SB[hf, :, at, :] = total.astype(jnp.bfloat16)
        for c in y_back(hf, p):
            c.start()

    scale = 1.0 / (pc * chans)

    def finish(hf, p):
        for c in y_back(hf, p):
            c.wait_recv()
        at = span_of(p)
        SR[hf, :, at, :] = (SR[hf, :, at, :] + SY[hf, :, at, :].astype(jnp.float32)) * scale
        gain = gain_ref[pl.ds(pl.multiple_of(mine * pc, pc), pc), :]

        def body(k, carry):
            n = (
                Nn[hf, k, mine].astype(jnp.float32)
                + RC[0, hf, k].astype(jnp.float32)
                + YR[hf, k].astype(jnp.float32)
            )
            st = X[hf, k, mine].astype(jnp.float32)
            s0 = SR[hf, 0, pl.ds(k, 1), :]
            s1 = SR[hf, 1, pl.ds(k, 1), :]
            out = (n * gain - s0 - st * s1) * INV[hf, pl.ds(k, 1), :]
            LR[hf, pl.ds(k, pc, stride=rows), :] = out
            return carry

        lax.fori_loop(p * piece, (p + 1) * piece, body, 0, unroll=4)

        def put(c, carry):
            rows_at = pl.ds(pl.multiple_of(c * rows + p * piece, piece), piece)
            pg_ref[hf, c, at, :] = LR[hf, rows_at, :].astype(jnp.bfloat16)
            return carry

        lax.fori_loop(0, pc, put, 0, unroll=4)

    items = [(hf, p) for hf in range(halves) for p in range(pieces)]

    def launch(hf, p):
        back(hf, p)
        for c in core_copies(hf, p):
            c.start()

    last = [(way, ch) for ch in range(CHUNKS) for way in ways_of(top, ch)]
    last += [(1 - way, ch) for way, ch in last]
    for p in range(pieces):
        run_near(p)
        if p > 0:
            combine(0, p - 1)
        if not cross:
            take = 1 if p + 1 < pieces else CHUNKS - p
            for way, ch in last[p : p + take]:
                forward(top, way, [ch])
        launch(0, p)
    for ch in range(CHUNKS):
        if not cross:
            for way, there in last[CHUNKS:]:
                if there == ch:
                    forward(top, way, [ch])
            for way in (0, 1):
                forward(top + 1, way, [ch])
        run_distant(ch)
        if ch == 0:
            combine(0, pieces - 1)
    for p in range(pieces):
        launch(1, p)
        finish(0, p)
        combine(1, p)

    allc = pc * chans
    wide = wt_ref[...].astype(jnp.float32)
    gain_term = jnp.sum(wide * WA[:, allc:], axis=0, keepdims=True)
    bias_term = jnp.sum(wide * jnp.sum(GA[...], axis=1, keepdims=True), axis=0, keepdims=True)
    sub = lax.broadcasted_iota(jnp.int32, (8, allc), 0)
    WS[me, : 4 * pc, :] = WA[:, :allc]
    WS[me, 4 * pc :, :] = jnp.where(sub == 0, gain_term, jnp.where(sub == 1, bias_term, 0.0))

    def wide_copy(hop):
        return remote(
            WS.at[me], WS.at[me], wbs.at[hop - 1], wbr.at[hop - 1], (me + hop) % ring, mine
        )

    for hop in range(1, ring):
        wide_copy(hop).start()

    for hop in range(1, ring):
        wide_copy(hop).wait_recv()
    summed = WS[0]
    for d in range(1, ring):
        summed = summed + WS[d]
    summed = summed * (1.0 / width)
    wsum_ref[...] = summed[: 4 * pc]
    VS[mine] = summed[4 * pc :]

    def vec_copy(hop):
        return remote(VS.at[mine], VS.at[mine], vs.at[hop - 1], vr.at[hop - 1], me, (mine + hop) % chans)

    for hop in range(1, chans):
        vec_copy(hop).start()
    for p in range(pieces):
        finish(1, p)
    for hop in range(1, chans):
        vec_copy(hop).wait_recv()
    total = VS[0]
    for d in range(1, chans):
        total = total + VS[d]
    vec_ref[...] = total

    windows(sends_window, lambda c: c.wait_send())
    for kind in range(len(rings)):
        for step in range(1, top + 1):
            for ch in range(CHUNKS):
                for way in ways_of(step, ch):
                    ring_sent(way, step, ch, kind)
        for way in (0, 1):
            @pl.when(chord_sends(way))
            def _(way=way, kind=kind):
                for ch in range(CHUNKS):
                    chord_copy(way, ch, kind).wait_send()
    for hf, p in items:
        for c in core_copies(hf, p) + y_back(hf, p):
            c.wait_send()
    for hop in range(1, ring):
        wide_copy(hop).wait_send()
    for hop in range(1, chans):
        vec_copy(hop).wait_send()


def call_mega(cross, dims, contact, act, cot, gates, gain, bias):
    chans, ring, pc, rows, piece, pieces, blk, width = dims
    allc = pc * chans
    bf, f32 = jnp.bfloat16, jnp.float32
    V, D = pltpu.VMEM, pltpu.SemaphoreType.DMA
    top, kinds = ring // 2, 2 if cross else 1
    scratch = [
        V((pc, rows, width), bf), V((pc, rows, width), bf),
        V((2, rows, chans, pc, blk), bf), V((2, rows, chans, pc, blk), bf),
        V((2, rows, 4 * pc, blk), f32), V((2, 2 * pc * rows, blk), f32), V((pc * rows, blk), f32),
        V((pc, ring * rows, blk), bf), V((pc, (ring if cross else 3) * rows, blk), bf),
        V((2, 2, rows, pc, blk), bf), V((2, rows, pc, blk), bf), V((2, rows, pc, blk), bf),
        V((2, rows, blk), f32), V((2, 2, rows, blk), f32), V((2, 2, rows, blk), f32),
        V((2, 2, rows, blk), bf), V((2, 2, rows, blk), bf),
        V((4 * pc, 2 * allc), f32), V((4 * pc, blk), f32),
        V((ring, 4 * pc + 8, allc), f32), V((chans, 8, allc), f32),
        V((4 * pc, allc), bf), V((allc, 4 * pc), bf), V((allc, blk), f32), V((allc, blk), f32),
        D((2,)), D((kinds, CHUNKS)), D((pieces,)), D((pieces,)), D((pieces,)), D((pieces,)), D((pieces,)), D((pieces,)),
        D((kinds, 2, top, CHUNKS)), D((kinds, 2, top, CHUNKS)), D((2, pieces)), D((2, pieces)),
        D((2, pieces, 2)), D((2, pieces, 2)), D((2, pieces)), D((2, pieces)),
        D((2, pieces)), D((2, pieces)), D((2, pieces)), D((2, pieces)),
        D((ring - 1,)), D((ring - 1,)), D((chans - 1,)), D((chans - 1,)),
    ]
    vmem = pl.BlockSpec(memory_space=pltpu.VMEM)
    hbm = pl.BlockSpec(memory_space=pl.ANY)
    return pl.pallas_call(
        functools.partial(mega, cross, dims),
        out_shape=(
            jax.ShapeDtypeStruct((2, pc, rows, blk), bf),
            jax.ShapeDtypeStruct((4 * pc, allc), f32),
            jax.ShapeDtypeStruct((8, allc), f32),
        ),
        in_specs=[pl.BlockSpec(memory_space=pltpu.SMEM), hbm, hbm] + [vmem] * 6,
        out_specs=(vmem, vmem, vmem),
        scratch_shapes=scratch,
        compiler_params=pltpu.CompilerParams(
            collective_id=2 if cross else 1, has_side_effects=True, vmem_limit_bytes=VMEM_BYTES
        ),
        name="triangle_cross" if cross else "triangle",
    )(contact, act, cot, *gates, gain, bias)


def expand(dims, contact_ref, pg_ref, wsum_ref, vec_ref, out_ref, g_ref, b_ref, *w_refs):
    chans, ring, pc, rows, piece, pieces, blk, width = dims
    row_first = lax.axis_index("rows") * rows
    for p in range(pieces):
        own = (row_first + p * piece) // blk
        at = pl.ds(p * piece, piece)
        near, far = pg_ref[0, :, at, :], pg_ref[1, :, at, :]
        none = jnp.zeros_like(near)
        for b in range(width // blk):
            held = jnp.where(contact_ref[own, b] > 0, far, none)
            out_ref[:, at, b * blk : (b + 1) * blk] = jnp.where(own == b, near, held)

    @pl.when(pl.program_id(0) == 0)
    def _():
        allc = pc * chans
        mine = lax.axis_index("chan")
        vec = pltpu.roll(vec_ref[...], (allc - mine * pc) % allc, 1)
        g_ref[...] = vec[0:1, :pc]
        b_ref[...] = vec[1:2, :pc]
        for i, ref in enumerate(w_refs):
            ref[...] = wsum_ref[i * pc : (i + 1) * pc, :]


def call_expand(dims, contact, pg, wsum, vec, steps=4):
    chans, ring, pc, rows, piece, pieces, blk, width = dims
    allc = pc * chans
    f32 = jnp.float32

    def whole(shape):
        return pl.BlockSpec(shape, lambda i: (0,) * len(shape))

    return pl.pallas_call(
        functools.partial(expand, dims),
        grid=(steps,),
        out_shape=(
            jax.ShapeDtypeStruct((pc, rows, width), pg.dtype),
            jax.ShapeDtypeStruct((1, pc), f32),
            jax.ShapeDtypeStruct((1, pc), f32),
        )
        + (jax.ShapeDtypeStruct((pc, allc), f32),) * 4,
        in_specs=[
            pl.BlockSpec(memory_space=pltpu.SMEM),
            pl.BlockSpec((2, pc // steps, rows, blk), lambda i: (0, i, 0, 0)),
            whole((4 * pc, allc)),
            whole((8, allc)),
        ],
        out_specs=(
            pl.BlockSpec((pc // steps, rows, width), lambda i: (i, 0, 0)),
            whole((1, pc)),
            whole((1, pc)),
        )
        + (whole((pc, allc)),) * 4,
        name="expand",
    )(contact, pg, wsum, vec)


def fused(
    pair_act, pair_cot, contact, ln_gain, ln_bias, left_gate, left_value, right_gate, right_value
):
    pc, rows, width = pair_act.shape
    blocks = contact.shape[0]
    blk = width // blocks
    chans, ring = lax.axis_size("chan"), lax.axis_size("rows")
    piece = math.gcd(rows, blk)
    pieces = rows // piece
    dims = (chans, ring, pc, rows, piece, pieces, blk, width)
    mutual = jnp.sum(contact * contact.T) > blocks
    gates = (left_gate.T, left_value.T, right_gate.T, right_value.T)
    args = (contact, pair_act, pair_cot, gates, ln_gain[None], ln_bias[None])
    held = lax.cond(
        mutual,
        lambda args: call_mega(True, dims, *args),
        lambda args: call_mega(False, dims, *args),
        args,
    )
    out = call_expand(dims, contact, *held)
    return (out[0], out[1][0], out[2][0]) + tuple(w.T for w in out[3:])


def local(*arrays):
    pc, rows, width = arrays[0].shape
    blk = width // arrays[2].shape[0]
    piece = math.gcd(rows, blk)
    chans, ring = lax.axis_size("chan"), lax.axis_size("rows")
    fits = (
        piece % 16 == 0 and rows // piece == 3 and blk == pc * chans == 4 * pc and ring == 8
    )
    return fused(*arrays) if fits else plain(*arrays)


def solution(mesh):
    in_specs = (
        P("chan", "rows", None),
        P("chan", "rows", None),
        P(),
        P(),
        P(),
        P(None, "chan"),
        P(None, "chan"),
        P(None, "chan"),
        P(None, "chan"),
    )
    out_specs = (
        P("chan", "rows", None),
        P("chan"),
        P("chan"),
        P(None, "chan"),
        P(None, "chan"),
        P(None, "chan"),
        P(None, "chan"),
    )
    return jax.shard_map(local, mesh=mesh, in_specs=in_specs, out_specs=out_specs, check_vma=False)
```
